512 devices in a mesh: dp: 16 (over x_hi, y, core), tensor: 32 (over z, x_lo).
Axes of the slice: x: 4 (x_hi: 2, x_lo: 2; x = x_hi * 2 + x_lo), y: 4, z: 16, core: 2. Of those that a mesh axis runs over, the one named last changes fastest.
Arguments:
- features: bfloat16 [8192, 16384], P('tensor', 'dp'), may hold values from -6 to 6
- up_blocks: bfloat16 [64, 128, 512], P('tensor', 'dp'), may hold values from -0.5 to 0.5
- down_blocks: bfloat16 [64, 512, 128], P('tensor', 'dp'), may hold values from -0.25 to 0.25
- out_cotangent: bfloat16 [8192, 16384], P('tensor', 'dp'), may hold values from -6 to 6
Outputs:
- mixed: bfloat16 [8192, 16384], P('tensor', 'dp')
- feature_grad: bfloat16 [8192, 16384], P('tensor', 'dp')
- up_grad: float32 [64, 128, 512], P('tensor', 'dp')
- down_grad: float32 [64, 512, 128], P('tensor', 'dp')
The draws below stay inside these ranges and needn't reach their ends.
All inputs are finite; a program needn't handle non-finite values.
Results may differ from the reference program's by a relative error of at most 0.023.
Values may be sent and summed in bfloat16 or wider, within the bound.
No kernel may reach another device: no remote copies, remote signals or barrier semaphores. Data moves between devices by JAX's collectives and lax.ppermute only.
A program may use at most 64 MiB of HBM per device.

```python
import jax
import jax.numpy as jnp
from jax import lax

NB = 64
BIN = 128
BOUT = 512
TOK_DEV = 1024
D = 8192
J_UP = 8
J_DN = 2
TOKENS = 16384


def block_scale(stream_key, dims, shards, low, largest):
    def one(position, blocks):
        draws = jax.random.uniform(jax.random.fold_in(jax.random.fold_in(stream_key, 6), position), (blocks,), jnp.float32, low / len(shards), largest / len(shards))
        return jnp.repeat(jnp.exp(draws), dims[position] // blocks).reshape((-1,) + (1,) * (len(dims) - position - 1))

    level = one(*shards[0])
    for cut in shards[1:]:
        level = level * one(*cut)
    return level


def centred(key, extent, width, reach, split=(), kind=jnp.bfloat16):
    gain = block_scale(key, extent, split, -0.22, 0.18) if split else 1.0
    entries = jax.random.normal(key, extent, jnp.float32) * width * gain
    return jnp.minimum(jnp.maximum(entries, -reach), reach).astype(kind)


def setup_inputs(seed: int = 0) -> dict:
    arg_keys = jax.random.split(jax.random.key(seed), 5)
    return {
        "features": centred(arg_keys[0], (D, TOKENS), 1.0, 6.0, ((0, 32), (1, 16))),
        "up_blocks": centred(arg_keys[1], (NB, BIN, BOUT), BIN ** -0.5, 0.5, ((0, 32), (1, 16))),
        "down_blocks": centred(arg_keys[2], (NB, BOUT, BIN), BOUT ** -0.5, 0.25, ((0, 32), (1, 16))),
        "out_cotangent": centred(arg_keys[3], (D, TOKENS), 1.0, 6.0, ((0, 32), (1, 16))),
    }


hp = lax.Precision.HIGHEST


def gelu_value(v):
    return 0.5 * v * (1.0 + lax.erf(v * 0.7071067811865476))


def gelu_slope(v):
    return 0.5 * (1.0 + lax.erf(v * 0.7071067811865476)) + v * jnp.exp(-0.5 * v * v) * 0.3989422804014327


def reference(features, up_blocks, down_blocks, out_cotangent):
    blocks = TOKENS // TOK_DEV
    up_f = up_blocks.astype(jnp.float32)
    down_f = down_blocks.astype(jnp.float32)
    xs = features.reshape(D, blocks, TOK_DEV).transpose(1, 0, 2)
    cs = out_cotangent.reshape(D, blocks, TOK_DEV).transpose(1, 0, 2)

    def step(carry, pair):
        grad_up, grad_down = carry
        x_blk, c_blk = pair
        xb = x_blk.reshape(NB, BIN, TOK_DEV)
        pre = jnp.einsum("bkn,bkt->bnt", up_f, xb.astype(jnp.float32), precision=hp).astype(jnp.bfloat16)
        permuted = pre.reshape(NB, NB, J_UP, TOK_DEV).transpose(1, 0, 2, 3).reshape(NB, BOUT, TOK_DEV)
        pf = permuted.astype(jnp.float32)
        act = gelu_value(pf).astype(jnp.bfloat16)
        blockout = jnp.einsum("gmc,gmt->gct", down_f, act.astype(jnp.float32), precision=hp).astype(jnp.bfloat16)
        mixed = blockout.reshape(NB, NB, J_DN, TOK_DEV).transpose(1, 0, 2, 3).reshape(D, TOK_DEV)
        dblock = c_blk.reshape(NB, NB, J_DN, TOK_DEV).transpose(1, 0, 2, 3).reshape(NB, BIN, TOK_DEV)
        dbf = dblock.astype(jnp.float32)
        dact = jnp.einsum("gmc,gct->gmt", down_f, dbf, precision=hp)
        dperm = (dact * gelu_slope(pf)).astype(jnp.bfloat16)
        grad_down = grad_down + jnp.einsum("gmt,gct->gmc", act.astype(jnp.float32), dbf, precision=hp)
        dpre = dperm.reshape(NB, NB, J_UP, TOK_DEV).transpose(1, 0, 2, 3).reshape(NB, BOUT, TOK_DEV)
        dpf = dpre.astype(jnp.float32)
        grad_up = grad_up + jnp.einsum("bkt,bnt->bkn", xb.astype(jnp.float32), dpf, precision=hp)
        fgrad = jnp.einsum("bkn,bnt->bkt", up_f, dpf, precision=hp).astype(jnp.bfloat16).reshape(D, TOK_DEV)
        return (grad_up, grad_down), (mixed, fgrad)

    init = (jnp.zeros((NB, BIN, BOUT), jnp.float32), jnp.zeros((NB, BOUT, BIN), jnp.float32))
    (grad_up, grad_down), (mixed, fgrad) = lax.scan(step, init, (xs, cs))
    mixed = mixed.transpose(1, 0, 2).reshape(D, TOKENS)
    fgrad = fgrad.transpose(1, 0, 2).reshape(D, TOKENS)
    return mixed, fgrad, grad_up, grad_down
```

```python
import jax
import jax.numpy as jnp
from jax import lax
from jax.sharding import PartitionSpec as P

NB = 64
BIN = 128
BOUT = 512
J_UP = 8
J_DN = 2
F32 = jnp.float32
BF16 = jnp.bfloat16


def gelu_value(v):
    return 0.5 * v * (1.0 + lax.erf(v * 0.7071067811865476))


def gelu_slope(v):
    return (
        0.5 * (1.0 + lax.erf(v * 0.7071067811865476))
        + v * jnp.exp(-0.5 * v * v) * 0.3989422804014327
    )


def exchange(x):
    return lax.all_to_all(x, "tensor", split_axis=0, concat_axis=0, tiled=True)


def gather_rows(up_blocks, down_blocks):
    n = lax.axis_size("dp")
    nb, ru, wu = up_blocks.shape
    rd, wd = down_blocks.shape[1:]
    both = jnp.concatenate([up_blocks, down_blocks.reshape(nb, ru, wu)], axis=0)
    sent = jnp.broadcast_to(both, (n,) + both.shape)
    got = lax.all_to_all(sent, "dp", split_axis=0, concat_axis=0, tiled=True)
    up = got[:, :nb].transpose(1, 0, 2, 3).reshape(nb, n * ru, wu)
    down = got[:, nb:].reshape(n, nb, rd, wd).transpose(1, 0, 2, 3).reshape(nb, n * rd, wd)
    return up, down


def sum_rows(up_term, down_term):
    n = lax.axis_size("dp")
    nb, hu, wu = up_term.shape
    hd, wd = down_term.shape[1:]
    ru, rd = hu // n, hd // n
    u = up_term.astype(BF16).reshape(nb, n, ru, wu).transpose(1, 0, 2, 3)
    d = down_term.astype(BF16).reshape(nb, n, ru, wu).transpose(1, 0, 2, 3)
    got = lax.all_to_all(
        jnp.concatenate([u, d], axis=1), "dp", split_axis=0, concat_axis=0, tiled=True
    )
    s = jnp.sum(got.astype(F32), axis=0)
    return s[:nb], s[nb:].reshape(nb, rd, wd)


def per_device(features, up_blocks, down_blocks, out_cotangent):
    nb = up_blocks.shape[0]
    t = features.shape[1]
    n = NB // nb
    up, down = gather_rows(up_blocks, down_blocks)
    x = features.reshape(nb, BIN, t)
    pre = jnp.einsum(
        "bkgj,bkt->gbjt", up.reshape(nb, BIN, NB, J_UP), x, preferred_element_type=F32
    ).astype(BF16)
    permuted = exchange(pre.reshape(n, nb, nb, J_UP, t))
    permuted = permuted.transpose(1, 0, 2, 3, 4).reshape(nb, BOUT, t)
    cot = out_cotangent.reshape(nb, n, nb, J_DN, t).transpose(1, 2, 0, 3, 4)
    dblock = exchange(cot).transpose(1, 0, 2, 3, 4).reshape(nb, BIN, t)
    pf = permuted.astype(F32)
    act = gelu_value(pf).astype(BF16)
    dact = jnp.einsum("gmc,gct->gmt", down, dblock, preferred_element_type=F32)
    dperm = (dact * gelu_slope(pf)).astype(BF16)
    dpre = exchange(dperm.reshape(nb, n, nb, J_UP, t).transpose(1, 2, 0, 3, 4))
    dpre = dpre.transpose(1, 0, 2, 3, 4).reshape(nb, BOUT, t)
    blockout = jnp.einsum("gmc,gmt->gct", down, act, preferred_element_type=F32).astype(BF16)
    mixed = exchange(blockout.reshape(nb, n, nb, J_DN, t).transpose(1, 2, 0, 3, 4))
    mixed = mixed.transpose(1, 0, 2, 3, 4).reshape(nb * BIN, t)
    down_term = jnp.einsum("gmt,gct->gmc", act, dblock, preferred_element_type=F32)
    up_term = jnp.einsum("bkt,bnt->bkn", x, dpre, preferred_element_type=F32)
    fgrad = jnp.einsum("bkn,bnt->bkt", up, dpre, preferred_element_type=F32).astype(BF16)
    up_grad, down_grad = sum_rows(up_term, down_term)
    return mixed, fgrad.reshape(nb * BIN, t), up_grad, down_grad


def solution(mesh):
    flat = P("tensor", "dp")
    rows = P("tensor", "dp", None)
    return jax.shard_map(
        per_device,
        mesh=mesh,
        in_specs=(flat, rows, rows, flat),
        out_specs=(flat, flat, rows, rows),
        check_vma=False,
    )
```

```python
import jax
import jax.numpy as jnp
from jax import lax
from jax.sharding import PartitionSpec as P

NB = 64
BIN = 128
BOUT = 512
J_UP = 8
J_DN = 2
F32 = jnp.float32
BF16 = jnp.bfloat16


def gelu_value(v):
    return 0.5 * v * (1.0 + lax.erf(v * 0.7071067811865476))


def gelu_slope(v):
    return (
        0.5 * (1.0 + lax.erf(v * 0.7071067811865476))
        + v * jnp.exp(-0.5 * v * v) * 0.3989422804014327
    )


DEVICES = ("dp", "tensor")


class Plan:
    def __init__(self):
        def index(xh, y, c, z, xl):
            return (((xh * 4 + y) * 2 + c) * 16 + z) * 2 + xl

        shuffle, mirror, weights, place = [], [], [], {}
        for z in range(16):
            for t in range(16):
                xh, y, c = t >> 3, (t >> 1) & 3, t & 1
                label = 8 * c + 4 * xh + y
                moved = (label + z) % 16
                c2, xh2, y2 = moved >> 3, (moved >> 2) & 1, moved & 3
                for xl in range(2):
                    xl2 = xl if xh2 == xh else 1 - xl
                    mid = index(xh2, y2, c2, z, xl2)
                    end = index(xh2, y2, c2, label, xl2)
                    shuffle.append((index(xh, y, c, z, xl), mid))
                    mirror.append((mid, end))
                    weights.append((index(xh2, y2, c2, z, xl), end))
                    place[label, 2 * z + xl] = end
        self.shuffle, self.mirror, self.weights = shuffle, mirror, weights
        self.layers = [[place[t, k] for k in range(32)] for t in range(16)]


PLAN = Plan()


def back(pairs):
    return [(b, a) for a, b in pairs]


def exchange(x):
    return lax.all_to_all(
        x, DEVICES, split_axis=0, concat_axis=0, tiled=True, axis_index_groups=PLAN.layers
    )


def to_work(x):
    return lax.ppermute(lax.ppermute(x, DEVICES, PLAN.shuffle), DEVICES, PLAN.mirror)


def to_store(x):
    return lax.ppermute(
        lax.ppermute(x, DEVICES, back(PLAN.mirror)), DEVICES, back(PLAN.shuffle)
    )


def gather_rows(up_blocks, down_blocks):
    n = lax.axis_size("dp")
    nb, ru, wu = up_blocks.shape
    rd, wd = down_blocks.shape[1:]
    both = jnp.concatenate([up_blocks, down_blocks.reshape(nb, ru, wu)], axis=0)
    sent = jnp.broadcast_to(both, (n,) + both.shape)
    got = lax.all_to_all(sent, "dp", split_axis=0, concat_axis=0, tiled=True)
    up = lax.ppermute(got[:, :nb], DEVICES, PLAN.weights)
    down = lax.ppermute(got[:, nb:], DEVICES, PLAN.weights)
    up = up.transpose(1, 0, 2, 3).reshape(nb, n * ru, wu)
    down = down.reshape(n, nb, rd, wd).transpose(1, 0, 2, 3).reshape(nb, n * rd, wd)
    return up, down


def sum_rows(up_term, down_term):
    n = lax.axis_size("dp")
    nb, hu, wu = up_term.shape
    hd, wd = down_term.shape[1:]
    ru, rd = hu // n, hd // n
    u = up_term.astype(BF16).reshape(nb, n, ru, wu).transpose(1, 0, 2, 3)
    d = down_term.astype(BF16).reshape(nb, n, ru, wu).transpose(1, 0, 2, 3)
    u = lax.ppermute(u, DEVICES, back(PLAN.weights))
    d = lax.ppermute(d, DEVICES, back(PLAN.weights))
    got = lax.all_to_all(
        jnp.concatenate([u, d], axis=1), "dp", split_axis=0, concat_axis=0, tiled=True
    )
    s = jnp.sum(got.astype(F32), axis=0)
    return s[:nb], s[nb:].reshape(nb, rd, wd)


def per_device(features, up_blocks, down_blocks, out_cotangent):
    nb = up_blocks.shape[0]
    t = features.shape[1]
    n = NB // nb
    up, down = gather_rows(up_blocks, down_blocks)
    x = to_work(features).reshape(nb, BIN, t)
    out_cotangent = to_work(out_cotangent)
    pre = jnp.einsum(
        "bkgj,bkt->gbjt", up.reshape(nb, BIN, NB, J_UP), x, preferred_element_type=F32
    ).astype(BF16)
    permuted = exchange(pre.reshape(n, nb, nb, J_UP, t))
    permuted = permuted.transpose(1, 0, 2, 3, 4).reshape(nb, BOUT, t)
    cot = out_cotangent.reshape(nb, n, nb, J_DN, t).transpose(1, 2, 0, 3, 4)
    dblock = exchange(cot).transpose(1, 0, 2, 3, 4).reshape(nb, BIN, t)
    pf = permuted.astype(F32)
    act = gelu_value(pf).astype(BF16)
    dact = jnp.einsum("gmc,gct->gmt", down, dblock, preferred_element_type=F32)
    dperm = (dact * gelu_slope(pf)).astype(BF16)
    dpre = exchange(dperm.reshape(nb, n, nb, J_UP, t).transpose(1, 2, 0, 3, 4))
    dpre = dpre.transpose(1, 0, 2, 3, 4).reshape(nb, BOUT, t)
    blockout = jnp.einsum("gmc,gmt->gct", down, act, preferred_element_type=F32).astype(BF16)
    mixed = exchange(blockout.reshape(nb, n, nb, J_DN, t).transpose(1, 2, 0, 3, 4))
    mixed = mixed.transpose(1, 0, 2, 3, 4).reshape(nb * BIN, t)
    down_term = jnp.einsum("gmt,gct->gmc", act, dblock, preferred_element_type=F32)
    up_term = jnp.einsum("bkt,bnt->bkn", x, dpre, preferred_element_type=F32)
    fgrad = jnp.einsum("bkn,bnt->bkt", up, dpre, preferred_element_type=F32).astype(BF16)
    up_grad, down_grad = sum_rows(up_term, down_term)
    return to_store(mixed), to_store(fgrad.reshape(nb * BIN, t)), up_grad, down_grad


def solution(mesh):
    flat = P("tensor", "dp")
    rows = P("tensor", "dp", None)
    return jax.shard_map(
        per_device,
        mesh=mesh,
        in_specs=(flat, rows, rows, flat),
        out_specs=(flat, flat, rows, rows),
        check_vma=False,
    )
```

```python
import jax
import jax.numpy as jnp
from jax import lax
from jax.sharding import PartitionSpec as P

NB = 64
BIN = 128
BOUT = 512
J_UP = 8
J_DN = 2
F32 = jnp.float32
BF16 = jnp.bfloat16


def gelu_value(v):
    return 0.5 * v * (1.0 + lax.erf(v * 0.7071067811865476))


def gelu_slope(v):
    return (
        0.5 * (1.0 + lax.erf(v * 0.7071067811865476))
        + v * jnp.exp(-0.5 * v * v) * 0.3989422804014327
    )


DEVICES = ("dp", "tensor")


class Plan:
    def __init__(self):
        def index(xh, y, c, z, xl):
            return (((xh * 4 + y) * 2 + c) * 16 + z) * 2 + xl

        shuffle, mirror, weights, place = [], [], [], {}
        for z in range(16):
            for t in range(16):
                xh, y, c = t >> 3, (t >> 1) & 3, t & 1
                label = 8 * c + 4 * xh + y
                moved = (label + z) % 16
                c2, xh2, y2 = moved >> 3, (moved >> 2) & 1, moved & 3
                for xl in range(2):
                    xl2 = xl if xh2 == xh else 1 - xl
                    mid = index(xh2, y2, c2, z, xl2)
                    end = index(xh2, y2, c2, label, xl2)
                    shuffle.append((index(xh, y, c, z, xl), mid))
                    mirror.append((mid, end))
                    weights.append((index(xh2, y2, c2, z, xl), end))
                    place[label, 2 * z + xl] = end
        self.shuffle, self.mirror, self.weights = shuffle, mirror, weights
        self.layers = [[place[t, k] for k in range(32)] for t in range(16)]


PLAN = Plan()


def back(pairs):
    return [(b, a) for a, b in pairs]


def exchange(x):
    return lax.all_to_all(
        x, DEVICES, split_axis=0, concat_axis=0, tiled=True, axis_index_groups=PLAN.layers
    )


def after(x, *others):
    return lax.optimization_barrier((x,) + others)[0]


def shuffle(x):
    return lax.ppermute(x, DEVICES, PLAN.shuffle)


def mirror(x):
    return lax.ppermute(x, DEVICES, PLAN.mirror)


def to_store(x):
    return lax.ppermute(
        lax.ppermute(x, DEVICES, back(PLAN.mirror)), DEVICES, back(PLAN.shuffle)
    )


def gather_rows(up_blocks, down_blocks):
    n = lax.axis_size("dp")
    nb, ru, wu = up_blocks.shape
    both = jnp.concatenate([up_blocks, down_blocks.reshape(nb, ru, wu)], axis=0)
    sent = jnp.broadcast_to(both, (n,) + both.shape)
    got = lax.all_to_all(sent, "dp", split_axis=0, concat_axis=0, tiled=True)
    return got[:, :nb], got[:, nb:]


def whole(rows, height, width):
    n, nb = rows.shape[:2]
    rows = lax.ppermute(rows, DEVICES, PLAN.weights)
    return rows.reshape(n, nb, height // n, width).transpose(1, 0, 2, 3).reshape(nb, height, width)


def sum_rows(up_term, down_term, gate):
    n = lax.axis_size("dp")
    nb, hu, wu = up_term.shape
    hd, wd = down_term.shape[1:]
    ru, rd = hu // n, hd // n
    u = up_term.astype(BF16).reshape(nb, n, ru, wu).transpose(1, 0, 2, 3)
    d = down_term.astype(BF16).reshape(nb, n, ru, wu).transpose(1, 0, 2, 3)
    u = lax.ppermute(u, DEVICES, back(PLAN.weights))
    d = lax.ppermute(d, DEVICES, back(PLAN.weights))
    both = after(jnp.concatenate([u, d], axis=1), gate)
    got = lax.all_to_all(both, "dp", split_axis=0, concat_axis=0, tiled=True)
    s = jnp.sum(got.astype(F32), axis=0)
    return s[:nb], s[nb:].reshape(nb, rd, wd)


def per_device(features, up_blocks, down_blocks, out_cotangent):
    nb = up_blocks.shape[0]
    t = features.shape[1]
    n = NB // nb
    moved = shuffle(features)
    up_rows, down_rows = gather_rows(up_blocks, down_blocks)
    moved_cot = shuffle(after(out_cotangent, moved, up_rows))
    x_flat = mirror(moved)
    up = whole(up_rows, BIN, BOUT)
    cot = mirror(after(moved_cot, x_flat))
    x = after(x_flat, moved_cot).reshape(nb, BIN, t)
    pre = jnp.einsum("bkn,bkt->bnt", up, x, preferred_element_type=F32).astype(BF16)
    permuted = exchange(pre.reshape(nb, n, nb, J_UP, t).transpose(1, 2, 0, 3, 4))
    down = whole(after(down_rows, up), BOUT, BIN)
    cot = after(cot, permuted).reshape(nb, n, nb, J_DN, t).transpose(1, 2, 0, 3, 4)
    dblock = exchange(cot)
    permuted = permuted.transpose(1, 0, 2, 3, 4).reshape(nb, BOUT, t)
    pf = permuted.astype(F32)
    act = gelu_value(pf).astype(BF16)
    blockout = jnp.einsum("gmc,gmt->gct", down, act, preferred_element_type=F32).astype(BF16)
    blockout = blockout.reshape(nb, n, nb, J_DN, t).transpose(1, 2, 0, 3, 4)
    mixed = exchange(after(blockout, dblock))
    dblock = dblock.transpose(1, 0, 2, 3, 4).reshape(nb, BIN, t)
    dact = jnp.einsum("gmc,gct->gmt", down, dblock, preferred_element_type=F32)
    dperm = (dact * gelu_slope(pf)).astype(BF16)
    dperm = dperm.reshape(nb, n, nb, J_UP, t).transpose(1, 2, 0, 3, 4)
    dpre = exchange(after(dperm, mixed))
    mixed = to_store(mixed.transpose(1, 0, 2, 3, 4).reshape(nb * BIN, t))
    down_term = jnp.einsum("gmt,gct->gmc", act, dblock, preferred_element_type=F32)
    dpre = dpre.transpose(1, 0, 2, 3, 4).reshape(nb, BOUT, t)
    fgrad = jnp.einsum("bkn,bnt->bkt", up, dpre, preferred_element_type=F32).astype(BF16)
    fgrad = fgrad.reshape(nb * BIN, t)
    dpre = after(dpre, fgrad)
    up_term = jnp.einsum("bkt,bnt->bkn", x, dpre, preferred_element_type=F32)
    fgrad = lax.ppermute(fgrad, DEVICES, back(PLAN.mirror))
    up_grad, down_grad = sum_rows(up_term, down_term, fgrad)
    fgrad = lax.ppermute(fgrad, DEVICES, back(PLAN.shuffle))
    return mixed, fgrad, up_grad, down_grad


def solution(mesh):
    flat = P("tensor", "dp")
    rows = P("tensor", "dp", None)
    return jax.shard_map(
        per_device,
        mesh=mesh,
        in_specs=(flat, rows, rows, flat),
        out_specs=(flat, flat, rows, rows),
        check_vma=False,
    )
```

```python
import jax
import jax.numpy as jnp
from jax import lax
from jax.sharding import PartitionSpec as P

NB = 64
BIN = 128
BOUT = 512
J_UP = 8
J_DN = 2
F32 = jnp.float32
BF16 = jnp.bfloat16


def gelu_value(v):
    return 0.5 * v * (1.0 + lax.erf(v * 0.7071067811865476))


def gelu_slope(v):
    return (
        0.5 * (1.0 + lax.erf(v * 0.7071067811865476))
        + v * jnp.exp(-0.5 * v * v) * 0.3989422804014327
    )


DEVICES = ("dp", "tensor")


class Plan:
    def __init__(self):
        def index(xh, y, c, z, xl):
            return (((xh * 4 + y) * 2 + c) * 16 + z) * 2 + xl

        def side(z, xh, xl):
            return xl if xh == (z >> 2) & 1 else 1 - xl

        def at(label):
            return (label >> 2) & 1, label & 3, label >> 3

        spots = [(z, *at(k), xl) for z in range(16) for k in range(16) for xl in range(2)]
        shuffle, mirror, place = [], [], {}
        for z in range(16):
            for label in range(16):
                xh, y, c = at(label)
                xh2, y2, c2 = at((label + z) % 16)
                for xl in range(2):
                    xl2 = side(label, xh2, xl)
                    mid = index(xh2, y2, c2, z, xl2)
                    end = index(xh2, y2, c2, label, xl2)
                    shuffle.append((index(xh, y, c, z, xl), mid))
                    mirror.append((mid, end))
                    place[label, 2 * z + xl] = end
        self.shuffle, self.mirror = shuffle, mirror
        self.layers = [[place[t, k] for k in range(32)] for t in range(16)]
        self.planes = [
            [index(*at(k), z, side(z, at(k)[0], xl)) for k in range(16)]
            for z in range(16)
            for xl in range(2)
        ]
        self.columns = [
            [index(*at(k), z, side(z, at(k)[0], xl)) for z in range(16)]
            for k in range(16)
            for xl in range(2)
        ]
        self.swap = [
            (index(xh, y, c, z, xl), index(xh, y, c, z, side(z, xh, xl)))
            for z, xh, y, c, xl in spots
        ]


PLAN = Plan()


def back(pairs):
    return [(b, a) for a, b in pairs]


def exchange(x, groups):
    return lax.all_to_all(
        x, DEVICES, split_axis=0, concat_axis=0, tiled=True, axis_index_groups=groups
    )


def roll(x, shift):
    return lax.dynamic_slice_in_dim(jnp.concatenate([x, x]), shift, x.shape[0])


def layer():
    return lax.axis_index("tensor") // 2


def after(x, *others):
    return lax.optimization_barrier((x,) + others)[0]


def shuffle(x):
    return lax.ppermute(x, DEVICES, PLAN.shuffle)


def mirror(x):
    return lax.ppermute(x, DEVICES, PLAN.mirror)


def unmirror(x):
    return lax.ppermute(x, DEVICES, back(PLAN.mirror))


def unshuffle(x):
    return lax.ppermute(x, DEVICES, back(PLAN.shuffle))


def gather_rows(up_blocks, down_blocks, gate):
    n = lax.axis_size("dp")
    nb, ru, wu = up_blocks.shape
    rd, wd = down_blocks.shape[1:]
    both = jnp.concatenate([up_blocks, down_blocks.reshape(nb, ru, wu)], axis=0)
    both = lax.ppermute(both, DEVICES, PLAN.swap)
    got = exchange(jnp.broadcast_to(both, (n,) + both.shape), PLAN.columns)
    got = exchange(roll(after(got, gate), n - layer()), PLAN.planes)
    got = got.reshape(2, 2, 4, 2 * nb, ru, wu).transpose(3, 1, 2, 0, 4, 5)
    up = got[:nb].reshape(nb, n * ru, wu)
    down = got[nb:].reshape(nb, n, rd, wd).reshape(nb, n * rd, wd)
    return up, down


def sum_rows(up_term, down_term, gate):
    n = lax.axis_size("dp")
    nb, hu, wu = up_term.shape
    hd, wd = down_term.shape[1:]
    ru, rd = hu // n, hd // n
    u = up_term.astype(BF16).reshape(nb, 2, 4, 2, ru, wu).transpose(3, 1, 2, 0, 4, 5)
    d = down_term.astype(BF16).reshape(nb, 2, 4, 2, ru, wu).transpose(3, 1, 2, 0, 4, 5)
    both = jnp.concatenate([u, d], axis=3).reshape(n, 2 * nb, ru, wu)
    got = roll(exchange(both, PLAN.planes), layer())
    s = jnp.sum(exchange(after(got, gate), PLAN.columns).astype(F32), axis=0)
    s = lax.ppermute(s, DEVICES, PLAN.swap)
    return s[:nb], s[nb:].reshape(nb, rd, wd)


def per_device(features, up_blocks, down_blocks, out_cotangent):
    nb = up_blocks.shape[0]
    t = features.shape[1]
    n = NB // nb
    x = mirror(shuffle(features))
    cot = mirror(shuffle(out_cotangent))
    up, down = gather_rows(up_blocks, down_blocks, x)
    x = x.reshape(nb, BIN, t)
    cot = cot.reshape(nb, n, nb, J_DN, t).transpose(1, 2, 0, 3, 4)
    pre = jnp.einsum("bkn,bkt->bnt", up, x, preferred_element_type=F32).astype(BF16)
    pre = pre.reshape(nb, n, nb, J_UP, t).transpose(1, 2, 0, 3, 4)
    sent = jnp.concatenate(
        [pre.reshape(n, nb * nb, J_UP, t), cot.reshape(n, 1, nb * nb * J_DN, t)], axis=1
    )
    got = exchange(sent, PLAN.layers)
    permuted = got[:, : nb * nb].reshape(n, nb, nb, J_UP, t)
    permuted = permuted.transpose(1, 0, 2, 3, 4).reshape(nb, BOUT, t)
    dblock = got[:, nb * nb].reshape(n, nb, nb, J_DN, t)
    dblock = dblock.transpose(1, 0, 2, 3, 4).reshape(nb, BIN, t)
    pf = permuted.astype(F32)
    act = gelu_value(pf).astype(BF16)
    blockout = jnp.einsum("gmc,gmt->gct", down, act, preferred_element_type=F32).astype(BF16)
    blockout = blockout.reshape(nb, n, nb, J_DN, t).transpose(1, 2, 0, 3, 4)
    mixed = exchange(blockout, PLAN.layers)
    dact = jnp.einsum("gmc,gct->gmt", down, dblock, preferred_element_type=F32)
    dperm = (dact * gelu_slope(pf)).astype(BF16)
    dperm = dperm.reshape(nb, n, nb, J_UP, t).transpose(1, 2, 0, 3, 4)
    dpre = exchange(after(dperm, mixed), PLAN.layers)
    mixed = unmirror(mixed.transpose(1, 0, 2, 3, 4).reshape(nb * BIN, t))
    down_term = jnp.einsum("gmt,gct->gmc", act, dblock, preferred_element_type=F32)
    dpre = after(dpre, mixed).transpose(1, 0, 2, 3, 4).reshape(nb, BOUT, t)
    fgrad = jnp.einsum("bkn,bnt->bkt", up, dpre, preferred_element_type=F32).astype(BF16)
    fgrad = fgrad.reshape(nb * BIN, t)
    dpre = after(dpre, fgrad)
    fgrad = unmirror(fgrad)
    up_term = jnp.einsum("bkt,bnt->bkn", x, dpre, preferred_element_type=F32)
    up_grad, down_grad = sum_rows(up_term, down_term, fgrad)
    return unshuffle(mixed), unshuffle(fgrad), up_grad, down_grad


def solution(mesh):
    flat = P("tensor", "dp")
    rows = P("tensor", "dp", None)
    return jax.shard_map(
        per_device,
        mesh=mesh,
        in_specs=(flat, rows, rows, flat),
        out_specs=(flat, flat, rows, rows),
        check_vma=False,
    )
```

```python
import jax
import jax.numpy as jnp
from jax import lax
from jax.sharding import PartitionSpec as P

NB = 64
BIN = 128
BOUT = 512
J_UP = 8
J_DN = 2
F32 = jnp.float32
BF16 = jnp.bfloat16


def gelu_value(v):
    return 0.5 * v * (1.0 + lax.erf(v * 0.7071067811865476))


def gelu_slope(v):
    return (
        0.5 * (1.0 + lax.erf(v * 0.7071067811865476))
        + v * jnp.exp(-0.5 * v * v) * 0.3989422804014327
    )


DEVICES = ("dp", "tensor")


def back(pairs):
    return [(b, a) for a, b in pairs]


class Plan:
    def __init__(self):
        def index(xh, y, c, z, xl):
            return (((xh * 4 + y) * 2 + c) * 16 + z) * 2 + xl

        shuffle, mirror, weights, place = [], [], [], {}
        for z in range(16):
            for t in range(16):
                xh, y, c = t >> 3, (t >> 1) & 3, t & 1
                label = 8 * c + 4 * xh + y
                moved = (label + z) % 16
                c2, xh2, y2 = moved >> 3, (moved >> 2) & 1, moved & 3
                for xl in range(2):
                    xl2 = xl if xh2 == xh else 1 - xl
                    mid = index(xh2, y2, c2, z, xl2)
                    end = index(xh2, y2, c2, label, xl2)
                    shuffle.append((index(xh, y, c, z, xl), mid))
                    mirror.append((mid, end))
                    weights.append((index(xh2, y2, c2, z, xl), end))
                    place[label, 2 * z + xl] = end
        self.shuffle, self.mirror, self.weights = shuffle, mirror, weights
        outward = dict(back(mirror)), dict(back(shuffle))
        self.home = [(end, outward[1][mid]) for end, mid in outward[0].items()]
        self.layers = [[place[t, k] for k in range(32)] for t in range(16)]


PLAN = Plan()


def exchange(x):
    return lax.all_to_all(
        x, DEVICES, split_axis=0, concat_axis=0, tiled=True, axis_index_groups=PLAN.layers
    )


def after(x, *others):
    return lax.optimization_barrier((x,) + others)[0]


def shuffle(x):
    return lax.ppermute(x, DEVICES, PLAN.shuffle)


def mirror(x):
    return lax.ppermute(x, DEVICES, PLAN.mirror)


def unmirror(x):
    return lax.ppermute(x, DEVICES, back(PLAN.mirror))


def unshuffle(x):
    return lax.ppermute(x, DEVICES, back(PLAN.shuffle))


def to_store(x):
    return lax.ppermute(x, DEVICES, PLAN.home)


def gather_rows(up_blocks, down_blocks):
    n = lax.axis_size("dp")
    nb, ru, wu = up_blocks.shape
    both = jnp.concatenate([up_blocks, down_blocks.reshape(nb, ru, wu)], axis=0)
    sent = jnp.broadcast_to(both, (n,) + both.shape)
    got = lax.all_to_all(sent, "dp", split_axis=0, concat_axis=0, tiled=True)
    return got[:, :nb], got[:, nb:]


def whole(rows, height, width):
    n, nb = rows.shape[:2]
    rows = lax.ppermute(rows, DEVICES, PLAN.weights)
    return rows.reshape(n, nb, height // n, width).transpose(1, 0, 2, 3).reshape(nb, height, width)


def sum_rows(up_term, down_term):
    n = lax.axis_size("dp")
    nb, hu, wu = up_term.shape
    hd, wd = down_term.shape[1:]
    ru, rd = hu // n, hd // n
    u = up_term.astype(BF16).reshape(nb, n, ru, wu).transpose(1, 0, 2, 3)
    d = down_term.astype(BF16).reshape(nb, n, ru, wu).transpose(1, 0, 2, 3)
    u = lax.ppermute(u, DEVICES, back(PLAN.weights))
    d = lax.ppermute(d, DEVICES, back(PLAN.weights))
    both = jnp.concatenate([u, d], axis=1)
    got = lax.all_to_all(both, "dp", split_axis=0, concat_axis=0, tiled=True)
    s = jnp.sum(got.astype(F32), axis=0)
    return s[:nb], s[nb:].reshape(nb, rd, wd)


def per_device(features, up_blocks, down_blocks, out_cotangent):
    nb = up_blocks.shape[0]
    t = features.shape[1]
    n = NB // nb
    moved = shuffle(features)
    cot = mirror(shuffle(out_cotangent))
    up_rows, down_rows = gather_rows(up_blocks, down_blocks)
    up = whole(up_rows, BIN, BOUT)
    x_flat = mirror(after(moved, cot))
    dblock = exchange(cot.reshape(nb, n, nb, J_DN, t).transpose(1, 2, 0, 3, 4))
    x = after(x_flat, dblock).reshape(nb, BIN, t)
    pre = jnp.einsum("bkn,bkt->bnt", up, x, preferred_element_type=F32).astype(BF16)
    permuted = exchange(pre.reshape(nb, n, nb, J_UP, t).transpose(1, 2, 0, 3, 4))
    down = whole(after(down_rows, x_flat), BOUT, BIN)
    permuted = permuted.transpose(1, 0, 2, 3, 4).reshape(nb, BOUT, t)
    pf = permuted.astype(F32)
    act = gelu_value(pf).astype(BF16)
    blockout = jnp.einsum("gmc,gmt->gct", down, act, preferred_element_type=F32).astype(BF16)
    blockout = blockout.reshape(nb, n, nb, J_DN, t).transpose(1, 2, 0, 3, 4)
    mixed = exchange(blockout)
    dblock = dblock.transpose(1, 0, 2, 3, 4).reshape(nb, BIN, t)
    dact = jnp.einsum("gmc,gct->gmt", down, dblock, preferred_element_type=F32)
    dperm = (dact * gelu_slope(pf)).astype(BF16)
    dperm = dperm.reshape(nb, n, nb, J_UP, t).transpose(1, 2, 0, 3, 4)
    dpre = exchange(after(dperm, mixed))
    mixed = unmirror(mixed.transpose(1, 0, 2, 3, 4).reshape(nb * BIN, t))
    down_term = jnp.einsum("gmt,gct->gmc", act, dblock, preferred_element_type=F32)
    dpre = after(dpre, mixed).transpose(1, 0, 2, 3, 4).reshape(nb, BOUT, t)
    fgrad = jnp.einsum("bkn,bnt->bkt", up, dpre, preferred_element_type=F32).astype(BF16)
    fgrad = fgrad.reshape(nb * BIN, t)
    dpre = after(dpre, fgrad)
    up_term = jnp.einsum("bkt,bnt->bkn", x, dpre, preferred_element_type=F32)
    up_grad, down_grad = sum_rows(up_term, down_term)
    return unshuffle(mixed), to_store(fgrad), up_grad, down_grad


def solution(mesh):
    flat = P("tensor", "dp")
    rows = P("tensor", "dp", None)
    return jax.shard_map(
        per_device,
        mesh=mesh,
        in_specs=(flat, rows, rows, flat),
        out_specs=(flat, flat, rows, rows),
        check_vma=False,
    )
```

```python
import jax
import jax.numpy as jnp
from jax import lax
from jax.sharding import PartitionSpec as P

NB = 64
BIN = 128
BOUT = 512
J_UP = 8
J_DN = 2
F32 = jnp.float32
BF16 = jnp.bfloat16


def gelu_value(v):
    return 0.5 * v * (1.0 + lax.erf(v * 0.7071067811865476))


def gelu_slope(v):
    return (
        0.5 * (1.0 + lax.erf(v * 0.7071067811865476))
        + v * jnp.exp(-0.5 * v * v) * 0.3989422804014327
    )


DEVICES = ("dp", "tensor")


def back(pairs):
    return [(b, a) for a, b in pairs]


class Plan:
    def __init__(self):
        def index(xh, y, c, z, xl):
            return (((xh * 4 + y) * 2 + c) * 16 + z) * 2 + xl

        shuffle, mirror, weights, place = [], [], [], {}
        for z in range(16):
            for t in range(16):
                xh, y, c = t >> 3, (t >> 1) & 3, t & 1
                label = 8 * c + 4 * xh + y
                moved = (label + z) % 16
                c2, xh2, y2 = moved >> 3, (moved >> 2) & 1, moved & 3
                for xl in range(2):
                    xl2 = xl if xh2 == xh else 1 - xl
                    mid = index(xh2, y2, c2, z, xl2)
                    end = index(xh2, y2, c2, label, xl2)
                    shuffle.append((index(xh, y, c, z, xl), mid))
                    mirror.append((mid, end))
                    weights.append((index(xh2, y2, c2, z, xl), end))
                    place[label, 2 * z + xl] = end
        self.shuffle, self.mirror, self.weights = shuffle, mirror, weights
        outward = dict(back(mirror)), dict(back(shuffle))
        self.home = [(end, outward[1][mid]) for end, mid in outward[0].items()]
        self.layers = [[place[t, k] for k in range(32)] for t in range(16)]


PLAN = Plan()


def exchange(x):
    return lax.all_to_all(
        x, DEVICES, split_axis=0, concat_axis=0, tiled=True, axis_index_groups=PLAN.layers
    )


def after(x, *others):
    return lax.optimization_barrier((x,) + others)[0]


def shuffle(x):
    return lax.ppermute(x, DEVICES, PLAN.shuffle)


def mirror(x):
    return lax.ppermute(x, DEVICES, PLAN.mirror)


def unmirror(x):
    return lax.ppermute(x, DEVICES, back(PLAN.mirror))


def unshuffle(x):
    return lax.ppermute(x, DEVICES, back(PLAN.shuffle))


def to_store(x):
    return lax.ppermute(x, DEVICES, PLAN.home)


def gather_rows(up_blocks, down_blocks):
    n = lax.axis_size("dp")
    nb, ru, wu = up_blocks.shape
    both = jnp.concatenate([up_blocks, down_blocks.reshape(nb, ru, wu)], axis=0)
    sent = jnp.broadcast_to(both, (n,) + both.shape)
    got = lax.all_to_all(sent, "dp", split_axis=0, concat_axis=0, tiled=True)
    return got[:, :nb], got[:, nb:]


def to_class(rows):
    return lax.ppermute(rows, DEVICES, PLAN.weights)


def from_class(rows):
    return lax.ppermute(rows, DEVICES, back(PLAN.weights))


def per_device(features, up_blocks, down_blocks, out_cotangent):
    nb, ru, wu = up_blocks.shape
    rd, wd = down_blocks.shape[1:]
    t = features.shape[1]
    n = NB // nb
    dp = lax.axis_size("dp")

    moved_cot = shuffle(out_cotangent)
    moved = shuffle(after(features, moved_cot)).reshape(nb, BIN, t)
    cot = mirror(moved_cot)
    up_rows, down_rows = gather_rows(up_blocks, down_blocks)

    def up_of(rows):
        return to_class(rows).reshape(BIN, BOUT)

    up0 = up_of(up_rows[:, 0])
    x0 = mirror(after(moved[0], cot))
    dblock = exchange(cot.reshape(nb, n, nb, J_DN, t).transpose(1, 2, 0, 3, 4))
    dblock = dblock.transpose(1, 0, 2, 3, 4).reshape(nb, BIN, t)
    down = to_class(after(down_rows, x0))
    x1 = mirror(after(moved[1], x0))
    up1 = up_of(after(up_rows[:, 1], x0))

    def pre_of(up, x):
        pre = jnp.einsum("kn,kt->nt", up, x, preferred_element_type=F32).astype(BF16)
        return pre.reshape(n, nb, J_UP, t)

    def hidden(got):
        v = got.transpose(1, 0, 2, 3).reshape(nb, n * J_UP, t).astype(F32)
        return v, gelu_value(v).astype(BF16)

    def backward(v, down):
        dact = jnp.einsum("gmc,gct->gmt", down, dblock, preferred_element_type=F32)
        dperm = (dact * gelu_slope(v)).astype(BF16)
        return dperm.reshape(nb, n, J_UP, t).transpose(1, 0, 2, 3)

    def grads(dpre, up, x):
        dpre = dpre.reshape(BOUT, t)
        fgrad = jnp.einsum("kn,nt->kt", up, dpre, preferred_element_type=F32).astype(BF16)
        dpre = after(dpre, fgrad)
        term = jnp.einsum("kt,nt->kn", x, dpre, preferred_element_type=F32)
        return fgrad, term.astype(BF16).reshape(dp, ru, wu)

    v0, act0 = hidden(exchange(pre_of(up0, after(x0, dblock))))
    down = down.reshape(dp, nb, rd, wd).transpose(1, 0, 2, 3).reshape(nb, n, nb, J_UP, wd)
    down0 = down[:, :, 0].reshape(nb, n * J_UP, wd)
    down1 = down[:, :, 1].reshape(nb, n * J_UP, wd)
    dpre0 = exchange(after(backward(v0, down0), x1))
    v1, act1 = hidden(exchange(after(pre_of(up1, x1), dpre0)))
    fgrad0, u0 = grads(dpre0, up0, x0)
    fgrad0 = to_store(fgrad0)
    u0 = from_class(u0)

    def down_product(down, act):
        return jnp.einsum("gmc,gmt->gct", down, act, preferred_element_type=F32)

    blockout = (down_product(down0, act0) + down_product(down1, act1)).astype(BF16)
    mixed = exchange(blockout.reshape(nb, n, nb, J_DN, t).transpose(1, 2, 0, 3, 4))

    def down_term(act):
        d = jnp.einsum("gmt,gct->gmc", act, dblock, preferred_element_type=F32)
        return d.astype(BF16).reshape(nb, n, 1, J_UP, wd)

    d = jnp.concatenate([down_term(act0), down_term(act1)], axis=2)
    d = from_class(d.reshape(nb, dp, ru, wu).transpose(1, 0, 2, 3))
    dpre1 = exchange(after(backward(v1, down1), mixed, fgrad0, u0))
    mixed = mixed.transpose(1, 0, 2, 3, 4).reshape(nb * BIN, t)
    mixed = unmirror(after(mixed, d))
    fgrad1, u1 = grads(dpre1, up1, x1)
    fgrad1 = to_store(fgrad1)
    u1 = from_class(after(u1, mixed))
    both = jnp.concatenate([u0[:, None], u1[:, None], d], axis=1)
    got = lax.all_to_all(both, "dp", split_axis=0, concat_axis=0, tiled=True)
    s = jnp.sum(got.astype(F32), axis=0)
    return (
        unshuffle(mixed),
        jnp.concatenate([fgrad0, fgrad1], axis=0),
        s[:nb],
        s[nb:].reshape(nb, rd, wd),
    )


def solution(mesh):
    flat = P("tensor", "dp")
    rows = P("tensor", "dp", None)
    return jax.shard_map(
        per_device,
        mesh=mesh,
        in_specs=(flat, rows, rows, flat),
        out_specs=(flat, flat, rows, rows),
        check_vma=False,
    )
```

```python
import jax
import jax.numpy as jnp
from jax import lax
from jax.sharding import PartitionSpec as P

NB = 64
BIN = 128
BOUT = 512
J_UP = 8
J_DN = 2
F32 = jnp.float32
BF16 = jnp.bfloat16


def gelu_value(v):
    return 0.5 * v * (1.0 + lax.erf(v * 0.7071067811865476))


def gelu_slope(v):
    return (
        0.5 * (1.0 + lax.erf(v * 0.7071067811865476))
        + v * jnp.exp(-0.5 * v * v) * 0.3989422804014327
    )


DEVICES = ("dp", "tensor")


def back(pairs):
    return [(b, a) for a, b in pairs]


class Plan:
    def __init__(self):
        def index(xh, y, c, z, xl):
            return (((xh * 4 + y) * 2 + c) * 16 + z) * 2 + xl

        def side(z, xh, xl):
            return xl if xh == (z >> 2) & 1 else 1 - xl

        def at(label):
            return (label >> 2) & 1, label & 3, label >> 3

        spots = [(z, *at(k), xl) for z in range(16) for k in range(16) for xl in range(2)]
        shuffle, mirror, weights, home, place = [], [], [], [], {}
        for z in range(16):
            for label in range(16):
                xh, y, c = at(label)
                xh2, y2, c2 = at((label + z) % 16)
                for xl in range(2):
                    xl2 = side(label, xh2, xl)
                    mid = index(xh2, y2, c2, z, xl2)
                    end = index(xh2, y2, c2, label, xl2)
                    shuffle.append((index(xh, y, c, z, xl), mid))
                    mirror.append((mid, end))
                    home.append((end, index(xh, y, c, z, xl)))
                    weights.append((index(xh2, y2, c2, z, xl), end))
                    place[label, 2 * z + xl] = end
        self.shuffle, self.mirror, self.home, self.weights = shuffle, mirror, home, weights
        self.layers = [[place[t, k] for k in range(32)] for t in range(16)]
        self.planes = [
            [index(*at(k), z, side(z, at(k)[0], xl)) for k in range(16)]
            for z in range(16)
            for xl in range(2)
        ]
        self.columns = [
            [index(*at(k), z, side(z, at(k)[0], xl)) for z in range(16)]
            for k in range(16)
            for xl in range(2)
        ]
        self.swap = [
            (index(xh, y, c, z, xl), index(xh, y, c, z, side(z, xh, xl)))
            for z, xh, y, c, xl in spots
        ]


PLAN = Plan()


def exchange(x, groups):
    return lax.all_to_all(
        x, DEVICES, split_axis=0, concat_axis=0, tiled=True, axis_index_groups=groups
    )


def roll(x, shift):
    return lax.dynamic_slice_in_dim(jnp.concatenate([x, x]), shift, x.shape[0])


def layer():
    return lax.axis_index("tensor") // 2


def after(x, *others):
    return lax.optimization_barrier((x,) + others)[0]


def shuffle(x):
    return lax.ppermute(x, DEVICES, PLAN.shuffle)


def mirror(x):
    return lax.ppermute(x, DEVICES, PLAN.mirror)


def unmirror(x):
    return lax.ppermute(x, DEVICES, back(PLAN.mirror))


def unshuffle(x):
    return lax.ppermute(x, DEVICES, back(PLAN.shuffle))


def to_store(x):
    return lax.ppermute(x, DEVICES, PLAN.home)


def gather_rows(up_blocks, down_blocks):
    n = lax.axis_size("dp")
    nb, ru, wu = up_blocks.shape
    rd, wd = down_blocks.shape[1:]
    both = jnp.concatenate([up_blocks, down_blocks.reshape(nb, ru, wu)], axis=0)
    both = lax.ppermute(both, DEVICES, PLAN.swap)
    got = lax.all_gather(both, DEVICES, axis_index_groups=PLAN.columns)
    got = exchange(roll(got, n - layer()), PLAN.planes)
    got = got.reshape(2, 2, 4, 2 * nb, ru, wu).transpose(3, 1, 2, 0, 4, 5)
    up = got[:nb].reshape(nb, n * ru, wu)
    down = got[nb:].reshape(nb, n, rd, wd).reshape(nb, n * rd, wd)
    return up, down


def to_rows(term):
    n = lax.axis_size("dp")
    nb = term.shape[0]
    rows = term.astype(BF16).reshape(nb, n, -1, BOUT).transpose(1, 0, 2, 3)
    return lax.ppermute(rows, DEVICES, back(PLAN.weights))


def sum_rows(up_term, down_term, down_shape):
    both = jnp.concatenate([up_term, down_term], axis=1)
    got = lax.all_to_all(both, "dp", split_axis=0, concat_axis=0, tiled=True)
    s = jnp.sum(got.astype(F32), axis=0)
    nb = down_shape[0]
    return s[:nb], s[nb:].reshape(down_shape)


def per_device(features, up_blocks, down_blocks, out_cotangent):
    nb = up_blocks.shape[0]
    t = features.shape[1]
    n = NB // nb
    moved = shuffle(features)
    moved_cot = shuffle(after(out_cotangent, moved))
    up, down = gather_rows(up_blocks, down_blocks)
    x_flat = mirror(moved)
    cot = mirror(after(moved_cot, x_flat))
    x = after(x_flat, moved_cot).reshape(nb, BIN, t)
    pre = jnp.einsum("bkn,bkt->bnt", up, x, preferred_element_type=F32).astype(BF16)
    permuted = exchange(pre.reshape(nb, n, nb, J_UP, t).transpose(1, 2, 0, 3, 4), PLAN.layers)
    cot = after(cot, permuted).reshape(nb, n, nb, J_DN, t).transpose(1, 2, 0, 3, 4)
    dblock = exchange(cot, PLAN.layers)
    permuted = permuted.transpose(1, 0, 2, 3, 4).reshape(nb, BOUT, t)
    pf = permuted.astype(F32)
    act = gelu_value(pf).astype(BF16)
    blockout = jnp.einsum("gmc,gmt->gct", down, act, preferred_element_type=F32).astype(BF16)
    blockout = blockout.reshape(nb, n, nb, J_DN, t).transpose(1, 2, 0, 3, 4)
    mixed = exchange(after(blockout, dblock), PLAN.layers)
    dblock = dblock.transpose(1, 0, 2, 3, 4).reshape(nb, BIN, t)
    dact = jnp.einsum("gmc,gct->gmt", down, dblock, preferred_element_type=F32)
    dperm = (dact * gelu_slope(pf)).astype(BF16)
    dperm = dperm.reshape(nb, n, nb, J_UP, t).transpose(1, 2, 0, 3, 4)
    down_term = jnp.einsum("gmt,gct->gmc", act, dblock, preferred_element_type=F32)
    down_term = to_rows(down_term)
    dpre = exchange(after(dperm, mixed, down_term), PLAN.layers)
    mixed = unmirror(mixed.transpose(1, 0, 2, 3, 4).reshape(nb * BIN, t))
    dpre = after(dpre, mixed).transpose(1, 0, 2, 3, 4).reshape(nb, BOUT, t)
    fgrad = jnp.einsum("bkn,bnt->bkt", up, dpre, preferred_element_type=F32).astype(BF16)
    fgrad = fgrad.reshape(nb * BIN, t)
    dpre = after(dpre, fgrad)
    up_term = jnp.einsum("bkt,bnt->bkn", x, dpre, preferred_element_type=F32)
    up_term = to_rows(up_term)
    up_grad, down_grad = sum_rows(up_term, down_term, down_blocks.shape)
    return unshuffle(after(mixed, up_term)), to_store(fgrad), up_grad, down_grad


def solution(mesh):
    flat = P("tensor", "dp")
    rows = P("tensor", "dp", None)
    return jax.shard_map(
        per_device,
        mesh=mesh,
        in_specs=(flat, rows, rows, flat),
        out_specs=(flat, flat, rows, rows),
        check_vma=False,
    )
```

```python
import jax
import jax.numpy as jnp
from jax import lax
from jax.sharding import PartitionSpec as P

NB = 64
BIN = 128
BOUT = 512
J_UP = 8
J_DN = 2
F32 = jnp.float32
BF16 = jnp.bfloat16


def gelu_value(v):
    return 0.5 * v * (1.0 + lax.erf(v * 0.7071067811865476))


def gelu_slope(v):
    return (
        0.5 * (1.0 + lax.erf(v * 0.7071067811865476))
        + v * jnp.exp(-0.5 * v * v) * 0.3989422804014327
    )


DEVICES = ("dp", "tensor")


def back(pairs):
    return [(b, a) for a, b in pairs]


class Plan:
    def __init__(self):
        def index(xh, y, c, z, xl):
            return (((xh * 4 + y) * 2 + c) * 16 + z) * 2 + xl

        shuffle, mirror, weights, place = [], [], [], {}
        for z in range(16):
            for t in range(16):
                xh, y, c = t >> 3, (t >> 1) & 3, t & 1
                label = 8 * c + 4 * xh + y
                moved = (label + z) % 16
                c2, xh2, y2 = moved >> 3, (moved >> 2) & 1, moved & 3
                for xl in range(2):
                    xl2 = xl if xh2 == xh else 1 - xl
                    mid = index(xh2, y2, c2, z, xl2)
                    end = index(xh2, y2, c2, label, xl2)
                    shuffle.append((index(xh, y, c, z, xl), mid))
                    mirror.append((mid, end))
                    weights.append((index(xh2, y2, c2, z, xl), end))
                    place[label, 2 * z + xl] = end
        self.shuffle, self.mirror, self.weights = shuffle, mirror, weights
        outward = dict(back(mirror)), dict(back(shuffle))
        self.home = [(end, outward[1][mid]) for end, mid in outward[0].items()]
        self.layers = [[place[t, k] for k in range(32)] for t in range(16)]


PLAN = Plan()


def exchange(x):
    return lax.all_to_all(
        x, DEVICES, split_axis=0, concat_axis=0, tiled=True, axis_index_groups=PLAN.layers
    )


def after(x, *others):
    return lax.optimization_barrier((x,) + others)[0]


def shuffle(x):
    return lax.ppermute(x, DEVICES, PLAN.shuffle)


def mirror(x):
    return lax.ppermute(x, DEVICES, PLAN.mirror)


def unmirror(x):
    return lax.ppermute(x, DEVICES, back(PLAN.mirror))


def unshuffle(x):
    return lax.ppermute(x, DEVICES, back(PLAN.shuffle))


def to_store(x):
    return lax.ppermute(x, DEVICES, PLAN.home)


def gather_rows(up_blocks, down_blocks):
    n = lax.axis_size("dp")
    nb, ru, wu = up_blocks.shape
    both = jnp.concatenate([up_blocks, down_blocks.reshape(nb, ru, wu)], axis=0)
    sent = jnp.broadcast_to(both, (n,) + both.shape)
    got = lax.all_to_all(sent, "dp", split_axis=0, concat_axis=0, tiled=True)
    return got[:, :nb], got[:, nb:]


def to_class(rows):
    return lax.ppermute(rows, DEVICES, PLAN.weights)


def whole(rows, height, width):
    n, nb = rows.shape[:2]
    return rows.reshape(n, nb, height // n, width).transpose(1, 0, 2, 3).reshape(nb, height, width)


def to_rows(term):
    n = lax.axis_size("dp")
    nb = term.shape[0]
    rows = term.astype(BF16).reshape(nb, n, -1, BOUT).transpose(1, 0, 2, 3)
    return lax.ppermute(rows, DEVICES, back(PLAN.weights))


def sum_rows(up_term, down_term, down_shape):
    both = jnp.concatenate([up_term, down_term], axis=1)
    got = lax.all_to_all(both, "dp", split_axis=0, concat_axis=0, tiled=True)
    s = jnp.sum(got.astype(F32), axis=0)
    nb = down_shape[0]
    return s[:nb], s[nb:].reshape(down_shape)


def per_device(features, up_blocks, down_blocks, out_cotangent):
    nb = up_blocks.shape[0]
    t = features.shape[1]
    n = NB // nb
    moved = shuffle(features)
    moved_cot = shuffle(out_cotangent)
    up_rows, down_rows = gather_rows(up_blocks, down_blocks)
    cot = mirror(after(moved_cot, up_rows))
    up_rows = to_class(up_rows)
    up = whole(up_rows, BIN, BOUT)
    x_flat = mirror(after(moved, cot))
    dblock = exchange(after(cot, up_rows).reshape(nb, n, nb, J_DN, t).transpose(1, 2, 0, 3, 4))
    x = after(x_flat, dblock).reshape(nb, BIN, t)
    pre = jnp.einsum("bkn,bkt->bnt", up, x, preferred_element_type=F32).astype(BF16)
    permuted = exchange(pre.reshape(nb, n, nb, J_UP, t).transpose(1, 2, 0, 3, 4))
    down = whole(to_class(after(down_rows, x_flat)), BOUT, BIN)
    permuted = permuted.transpose(1, 0, 2, 3, 4).reshape(nb, BOUT, t)
    pf = permuted.astype(F32)
    act = gelu_value(pf).astype(BF16)
    blockout = jnp.einsum("gmc,gmt->gct", down, act, preferred_element_type=F32).astype(BF16)
    blockout = blockout.reshape(nb, n, nb, J_DN, t).transpose(1, 2, 0, 3, 4)
    mixed = exchange(blockout)
    dblock = dblock.transpose(1, 0, 2, 3, 4).reshape(nb, BIN, t)
    dact = jnp.einsum("gmc,gct->gmt", down, dblock, preferred_element_type=F32)
    dperm = (dact * gelu_slope(pf)).astype(BF16)
    dperm = dperm.reshape(nb, n, nb, J_UP, t).transpose(1, 2, 0, 3, 4)
    dpre = exchange(after(dperm, mixed))
    mixed = unmirror(mixed.transpose(1, 0, 2, 3, 4).reshape(nb * BIN, t))
    down_term = jnp.einsum("gmt,gct->gmc", act, dblock, preferred_element_type=F32)
    dpre = dpre.transpose(1, 0, 2, 3, 4).reshape(nb, BOUT, t)
    fgrad = jnp.einsum("bkn,bnt->bkt", up, dpre, preferred_element_type=F32).astype(BF16)
    fgrad = fgrad.reshape(nb * BIN, t)
    dpre = after(dpre, fgrad, mixed)
    up_term = jnp.einsum("bkt,bnt->bkn", x, dpre, preferred_element_type=F32)
    up_term = to_rows(up_term)
    up_grad, down_grad = sum_rows(up_term, to_rows(down_term), down_blocks.shape)
    return unshuffle(after(mixed, up_term)), to_store(fgrad), up_grad, down_grad


def solution(mesh):
    flat = P("tensor", "dp")
    rows = P("tensor", "dp", None)
    return jax.shard_map(
        per_device,
        mesh=mesh,
        in_specs=(flat, rows, rows, flat),
        out_specs=(flat, flat, rows, rows),
        check_vma=False,
    )
```

```python
import jax
import jax.numpy as jnp
from jax import lax
from jax.sharding import PartitionSpec as P

NB = 64
BIN = 128
BOUT = 512
J_UP = 8
J_DN = 2
F32 = jnp.float32
BF16 = jnp.bfloat16


def gelu_value(v):
    return 0.5 * v * (1.0 + lax.erf(v * 0.7071067811865476))


def gelu_slope(v):
    return (
        0.5 * (1.0 + lax.erf(v * 0.7071067811865476))
        + v * jnp.exp(-0.5 * v * v) * 0.3989422804014327
    )


DEVICES = ("dp", "tensor")


def back(pairs):
    return [(b, a) for a, b in pairs]


class Plan:
    def __init__(self):
        def index(xh, y, c, z, xl):
            return (((xh * 4 + y) * 2 + c) * 16 + z) * 2 + xl

        shuffle, mirror, weights, place = [], [], [], {}
        for z in range(16):
            for t in range(16):
                xh, y, c = t >> 3, (t >> 1) & 3, t & 1
                label = 8 * c + 4 * xh + y
                moved = (label + z) % 16
                c2, xh2, y2 = moved >> 3, (moved >> 2) & 1, moved & 3
                for xl in range(2):
                    xl2 = xl if xh2 == xh else 1 - xl
                    mid = index(xh2, y2, c2, z, xl2)
                    end = index(xh2, y2, c2, label, xl2)
                    shuffle.append((index(xh, y, c, z, xl), mid))
                    mirror.append((mid, end))
                    weights.append((index(xh2, y2, c2, z, xl), end))
                    place[label, 2 * z + xl] = end
        self.shuffle, self.mirror, self.weights = shuffle, mirror, weights
        outward = dict(back(mirror)), dict(back(shuffle))
        self.home = [(end, outward[1][mid]) for end, mid in outward[0].items()]
        self.layers = [[place[t, k] for k in range(32)] for t in range(16)]


PLAN = Plan()


def exchange(x):
    return lax.all_to_all(
        x, DEVICES, split_axis=0, concat_axis=0, tiled=True, axis_index_groups=PLAN.layers
    )


def after(x, *others):
    return lax.optimization_barrier((x,) + others)[0]


def shuffle(x):
    return lax.ppermute(x, DEVICES, PLAN.shuffle)


def mirror(x):
    return lax.ppermute(x, DEVICES, PLAN.mirror)


def unmirror(x):
    return lax.ppermute(x, DEVICES, back(PLAN.mirror))


def unshuffle(x):
    return lax.ppermute(x, DEVICES, back(PLAN.shuffle))


def to_store(x):
    return lax.ppermute(x, DEVICES, PLAN.home)


def gather_rows(up_blocks, down_blocks):
    n = lax.axis_size("dp")
    nb, ru, wu = up_blocks.shape
    both = jnp.concatenate([up_blocks, down_blocks.reshape(nb, ru, wu)], axis=0)
    sent = jnp.broadcast_to(both, (n,) + both.shape)
    got = lax.all_to_all(sent, "dp", split_axis=0, concat_axis=0, tiled=True)
    return got[:, :nb], got[:, nb:]


def whole(rows, height, width):
    n, nb = rows.shape[:2]
    rows = lax.ppermute(rows, DEVICES, PLAN.weights)
    return rows.reshape(n, nb, height // n, width).transpose(1, 0, 2, 3).reshape(nb, height, width)


def to_rows(term):
    n = lax.axis_size("dp")
    nb = term.shape[0]
    rows = term.astype(BF16).reshape(nb, n, -1, BOUT).transpose(1, 0, 2, 3)
    return lax.ppermute(rows, DEVICES, back(PLAN.weights))


def sum_rows(up_term, down_term, down_shape):
    both = jnp.concatenate([up_term, down_term], axis=1)
    got = lax.all_to_all(both, "dp", split_axis=0, concat_axis=0, tiled=True)
    s = jnp.sum(got.astype(F32), axis=0)
    nb = down_shape[0]
    return s[:nb], s[nb:].reshape(down_shape)


def per_device(features, up_blocks, down_blocks, out_cotangent):
    nb = up_blocks.shape[0]
    t = features.shape[1]
    n = NB // nb
    moved = shuffle(features)
    cot = mirror(shuffle(out_cotangent))
    up_rows, down_rows = gather_rows(up_blocks, down_blocks)
    up = whole(up_rows, BIN, BOUT)
    x_flat = mirror(after(moved, cot))
    dblock = exchange(cot.reshape(nb, n, nb, J_DN, t).transpose(1, 2, 0, 3, 4))
    x = after(x_flat, dblock).reshape(nb, BIN, t)
    pre = jnp.einsum("bkn,bkt->bnt", up, x, preferred_element_type=F32).astype(BF16)
    permuted = exchange(pre.reshape(nb, n, nb, J_UP, t).transpose(1, 2, 0, 3, 4))
    down = whole(after(down_rows, x_flat), BOUT, BIN)
    permuted = permuted.transpose(1, 0, 2, 3, 4).reshape(nb, BOUT, t)
    pf = permuted.astype(F32)
    dblock = dblock.transpose(1, 0, 2, 3, 4).reshape(nb, BIN, t)
    dact = jnp.einsum("gmc,gct->gmt", down, dblock, preferred_element_type=F32)
    dperm = (dact * gelu_slope(pf)).astype(BF16)
    dpre = exchange(dperm.reshape(nb, n, nb, J_UP, t).transpose(1, 2, 0, 3, 4))
    act = gelu_value(pf).astype(BF16)
    down_term = to_rows(jnp.einsum("gmt,gct->gmc", act, dblock, preferred_element_type=F32))
    blockout = jnp.einsum("gmc,gmt->gct", down, act, preferred_element_type=F32).astype(BF16)
    blockout = blockout.reshape(nb, n, nb, J_DN, t).transpose(1, 2, 0, 3, 4)
    mixed = exchange(after(blockout, dpre, down_term))
    dpre = dpre.transpose(1, 0, 2, 3, 4).reshape(nb, BOUT, t)
    fgrad = jnp.einsum("bkn,bnt->bkt", up, dpre, preferred_element_type=F32).astype(BF16)
    fgrad = unmirror(fgrad.reshape(nb * BIN, t))
    up_term = to_rows(jnp.einsum("bkt,bnt->bkn", x, dpre, preferred_element_type=F32))
    mixed = mixed.transpose(1, 0, 2, 3, 4).reshape(nb * BIN, t)
    mixed = to_store(after(mixed, fgrad))
    up_grad, down_grad = sum_rows(up_term, down_term, down_blocks.shape)
    return mixed, unshuffle(fgrad), up_grad, down_grad


def solution(mesh):
    flat = P("tensor", "dp")
    rows = P("tensor", "dp", None)
    return jax.shard_map(
        per_device,
        mesh=mesh,
        in_specs=(flat, rows, rows, flat),
        out_specs=(flat, flat, rows, rows),
        check_vma=False,
    )
```

```python
import jax
import jax.numpy as jnp
from jax import lax
from jax.sharding import PartitionSpec as P

NB = 64
BIN = 128
BOUT = 512
J_UP = 8
J_DN = 2
F32 = jnp.float32
BF16 = jnp.bfloat16


def gelu_value(v):
    return 0.5 * v * (1.0 + lax.erf(v * 0.7071067811865476))


def gelu_slope(v):
    return (
        0.5 * (1.0 + lax.erf(v * 0.7071067811865476))
        + v * jnp.exp(-0.5 * v * v) * 0.3989422804014327
    )


DEVICES = ("dp", "tensor")


def back(pairs):
    return [(b, a) for a, b in pairs]


class Plan:
    def __init__(self):
        def index(xh, y, c, z, xl):
            return (((xh * 4 + y) * 2 + c) * 16 + z) * 2 + xl

        shuffle, mirror, weights, place = [], [], [], {}
        for z in range(16):
            for t in range(16):
                xh, y, c = t >> 3, (t >> 1) & 3, t & 1
                label = 8 * c + 4 * xh + y
                moved = (label + z) % 16
                c2, xh2, y2 = moved >> 3, (moved >> 2) & 1, moved & 3
                for xl in range(2):
                    xl2 = xl if xh2 == xh else 1 - xl
                    mid = index(xh2, y2, c2, z, xl2)
                    end = index(xh2, y2, c2, label, xl2)
                    shuffle.append((index(xh, y, c, z, xl), mid))
                    mirror.append((mid, end))
                    weights.append((index(xh2, y2, c2, z, xl), end))
                    place[label, 2 * z + xl] = end
        self.shuffle, self.mirror, self.weights = shuffle, mirror, weights
        outward = dict(back(mirror)), dict(back(shuffle))
        self.home = [(end, outward[1][mid]) for end, mid in outward[0].items()]
        self.layers = [[place[t, k] for k in range(32)] for t in range(16)]


PLAN = Plan()


def exchange(x):
    return lax.all_to_all(
        x, DEVICES, split_axis=0, concat_axis=0, tiled=True, axis_index_groups=PLAN.layers
    )


def after(x, *others):
    return lax.optimization_barrier((x,) + others)[0]


def shuffle(x):
    return lax.ppermute(x, DEVICES, PLAN.shuffle)


def mirror(x):
    return lax.ppermute(x, DEVICES, PLAN.mirror)


def unmirror(x):
    return lax.ppermute(x, DEVICES, back(PLAN.mirror))


def unshuffle(x):
    return lax.ppermute(x, DEVICES, back(PLAN.shuffle))


def to_store(x):
    return lax.ppermute(x, DEVICES, PLAN.home)


def gather_rows(up_blocks, down_blocks):
    n = lax.axis_size("dp")
    nb, ru, wu = up_blocks.shape
    both = jnp.concatenate([up_blocks, down_blocks.reshape(nb, ru, wu)], axis=0)
    sent = jnp.broadcast_to(both, (n,) + both.shape)
    got = lax.all_to_all(sent, "dp", split_axis=0, concat_axis=0, tiled=True)
    return got[:, :nb], got[:, nb:]


def whole(rows, height, width):
    n, nb = rows.shape[:2]
    rows = lax.ppermute(rows, DEVICES, PLAN.weights)
    return rows.reshape(n, nb, height // n, width).transpose(1, 0, 2, 3).reshape(nb, height, width)


def to_rows(term):
    n = lax.axis_size("dp")
    nb = term.shape[0]
    rows = term.astype(BF16).reshape(nb, n, -1, BOUT).transpose(1, 0, 2, 3)
    return lax.ppermute(rows, DEVICES, back(PLAN.weights))


def sum_rows(up_term, down_term, down_shape):
    both = jnp.concatenate([up_term, down_term], axis=1)
    got = lax.all_to_all(both, "dp", split_axis=0, concat_axis=0, tiled=True)
    s = jnp.sum(got.astype(F32), axis=0)
    nb = down_shape[0]
    return s[:nb], s[nb:].reshape(down_shape)


def per_device(features, up_blocks, down_blocks, out_cotangent):
    nb = up_blocks.shape[0]
    t = features.shape[1]
    n = NB // nb
    moved = shuffle(features)
    cot = mirror(shuffle(out_cotangent))
    up_rows, down_rows = gather_rows(up_blocks, down_blocks)
    up = whole(up_rows, BIN, BOUT)
    x_flat = mirror(after(moved, cot))
    dblock = exchange(cot.reshape(nb, n, nb, J_DN, t).transpose(1, 2, 0, 3, 4))
    x = after(x_flat, dblock).reshape(nb, BIN, t)
    pre = jnp.einsum("bkn,bkt->bnt", up, x, preferred_element_type=F32).astype(BF16)
    permuted = exchange(pre.reshape(nb, n, nb, J_UP, t).transpose(1, 2, 0, 3, 4))
    down = whole(after(down_rows, x_flat), BOUT, BIN)
    permuted = permuted.transpose(1, 0, 2, 3, 4).reshape(nb, BOUT, t)
    pf = permuted.astype(F32)
    dblock = dblock.transpose(1, 0, 2, 3, 4).reshape(nb, BIN, t)
    dact = jnp.einsum("gmc,gct->gmt", down, dblock, preferred_element_type=F32)
    dperm = (dact * gelu_slope(pf)).astype(BF16)
    dpre = exchange(dperm.reshape(nb, n, nb, J_UP, t).transpose(1, 2, 0, 3, 4))
    act = gelu_value(pf).astype(BF16)
    down_term = to_rows(jnp.einsum("gmt,gct->gmc", act, dblock, preferred_element_type=F32))
    blockout = jnp.einsum("gmc,gmt->gct", down, act, preferred_element_type=F32).astype(BF16)
    blockout = blockout.reshape(nb, n, nb, J_DN, t).transpose(1, 2, 0, 3, 4)
    mixed = exchange(after(blockout, dpre, down_term))
    dpre = dpre.transpose(1, 0, 2, 3, 4).reshape(nb, BOUT, t)
    fgrad = jnp.einsum("bkn,bnt->bkt", up, dpre, preferred_element_type=F32).astype(BF16)
    fgrad = unmirror(fgrad.reshape(nb * BIN, t))
    up_term = jnp.einsum("bkt,bnt->bkn", x, dpre, preferred_element_type=F32).astype(BF16)
    up_term = to_rows(after(up_term, mixed))
    mixed = mixed.transpose(1, 0, 2, 3, 4).reshape(nb * BIN, t)
    mixed = to_store(mixed)
    up_grad, down_grad = sum_rows(after(up_term, fgrad), down_term, down_blocks.shape)
    return mixed, unshuffle(fgrad), up_grad, down_grad


def solution(mesh):
    flat = P("tensor", "dp")
    rows = P("tensor", "dp", None)
    return jax.shard_map(
        per_device,
        mesh=mesh,
        in_specs=(flat, rows, rows, flat),
        out_specs=(flat, flat, rows, rows),
        check_vma=False,
    )
```

```python
import jax
import jax.numpy as jnp
from jax import lax
from jax.sharding import PartitionSpec as P

NB = 64
BIN = 128
BOUT = 512
J_UP = 8
J_DN = 2
F32 = jnp.float32
BF16 = jnp.bfloat16


def gelu_value(v):
    return 0.5 * v * (1.0 + lax.erf(v * 0.7071067811865476))


def gelu_slope(v):
    return (
        0.5 * (1.0 + lax.erf(v * 0.7071067811865476))
        + v * jnp.exp(-0.5 * v * v) * 0.3989422804014327
    )


DEVICES = ("dp", "tensor")


def back(pairs):
    return [(b, a) for a, b in pairs]


class Plan:
    def __init__(self):
        def index(xh, y, c, z, xl):
            return (((xh * 4 + y) * 2 + c) * 16 + z) * 2 + xl

        shuffle, mirror, weights, place = [], [], [], {}
        for z in range(16):
            for t in range(16):
                xh, y, c = t >> 3, (t >> 1) & 3, t & 1
                label = 8 * c + 4 * xh + y
                moved = (label + z) % 16
                c2, xh2, y2 = moved >> 3, (moved >> 2) & 1, moved & 3
                for xl in range(2):
                    xl2 = xl if xh2 == xh else 1 - xl
                    mid = index(xh2, y2, c2, z, xl2)
                    end = index(xh2, y2, c2, label, xl2)
                    shuffle.append((index(xh, y, c, z, xl), mid))
                    mirror.append((mid, end))
                    weights.append((index(xh2, y2, c2, z, xl), end))
                    place[label, 2 * z + xl] = end
        self.shuffle, self.mirror, self.weights = shuffle, mirror, weights
        outward = dict(back(mirror)), dict(back(shuffle))
        self.home = [(end, outward[1][mid]) for end, mid in outward[0].items()]
        self.layers = [[place[t, k] for k in range(32)] for t in range(16)]


PLAN = Plan()


def exchange(x):
    return lax.all_to_all(
        x, DEVICES, split_axis=0, concat_axis=0, tiled=True, axis_index_groups=PLAN.layers
    )


def after(x, *others):
    return lax.optimization_barrier((x,) + others)[0]


def shuffle(x):
    return lax.ppermute(x, DEVICES, PLAN.shuffle)


def mirror(x):
    return lax.ppermute(x, DEVICES, PLAN.mirror)


def to_store(x):
    return lax.ppermute(x, DEVICES, PLAN.home)


def gather_rows(up_blocks, down_blocks):
    n = lax.axis_size("dp")
    nb, ru, wu = up_blocks.shape
    both = jnp.concatenate([up_blocks, down_blocks.reshape(nb, ru, wu)], axis=0)
    sent = jnp.broadcast_to(both, (n,) + both.shape)
    got = lax.all_to_all(sent, "dp", split_axis=0, concat_axis=0, tiled=True)
    return got[:, :nb], got[:, nb:]


def whole(rows, height, width):
    n, nb = rows.shape[:2]
    rows = lax.ppermute(rows, DEVICES, PLAN.weights)
    return rows.reshape(n, nb, height // n, width).transpose(1, 0, 2, 3).reshape(nb, height, width)


def to_rows(term):
    n = lax.axis_size("dp")
    nb = term.shape[0]
    rows = term.astype(BF16).reshape(nb, n, -1, BOUT).transpose(1, 0, 2, 3)
    return lax.ppermute(rows, DEVICES, back(PLAN.weights))


def sum_rows(up_term, down_term, down_shape):
    both = jnp.concatenate([up_term, down_term], axis=1)
    got = lax.all_to_all(both, "dp", split_axis=0, concat_axis=0, tiled=True)
    s = jnp.sum(got.astype(F32), axis=0)
    nb = down_shape[0]
    return s[:nb], s[nb:].reshape(down_shape)


def per_device(features, up_blocks, down_blocks, out_cotangent):
    nb = up_blocks.shape[0]
    t = features.shape[1]
    n = NB // nb
    moved = shuffle(features)
    cot = mirror(shuffle(out_cotangent))
    up_rows, down_rows = gather_rows(up_blocks, down_blocks)
    up = whole(up_rows, BIN, BOUT)
    x_flat = mirror(after(moved, cot))
    dblock = exchange(cot.reshape(nb, n, nb, J_DN, t).transpose(1, 2, 0, 3, 4))
    x = after(x_flat, dblock).reshape(nb, BIN, t)
    pre = jnp.einsum("bkn,bkt->bnt", up, x, preferred_element_type=F32).astype(BF16)
    permuted = exchange(pre.reshape(nb, n, nb, J_UP, t).transpose(1, 2, 0, 3, 4))
    down = whole(after(down_rows, x_flat), BOUT, BIN)
    permuted = permuted.transpose(1, 0, 2, 3, 4).reshape(nb, BOUT, t)
    pf = permuted.astype(F32)
    dblock = dblock.transpose(1, 0, 2, 3, 4).reshape(nb, BIN, t)
    dact = jnp.einsum("gmc,gct->gmt", down, dblock, preferred_element_type=F32)
    dperm = (dact * gelu_slope(pf)).astype(BF16)
    dpre = exchange(dperm.reshape(nb, n, nb, J_UP, t).transpose(1, 2, 0, 3, 4))
    act = gelu_value(pf).astype(BF16)
    down_term = jnp.einsum("gmt,gct->gmc", act, dblock, preferred_element_type=F32).astype(BF16)
    early = to_rows(down_term[:1])
    blockout = jnp.einsum("gmc,gmt->gct", down, act, preferred_element_type=F32).astype(BF16)
    blockout = blockout.reshape(nb, n, nb, J_DN, t).transpose(1, 2, 0, 3, 4)
    mixed = exchange(after(blockout, dpre, early))
    dpre = dpre.transpose(1, 0, 2, 3, 4).reshape(nb, BOUT, t)
    fgrad = jnp.einsum("bkn,bnt->bkt", up, dpre, preferred_element_type=F32).astype(BF16)
    fgrad = to_store(fgrad.reshape(nb * BIN, t))
    up_term = to_rows(jnp.einsum("bkt,bnt->bkn", x, dpre, preferred_element_type=F32))
    mixed = mixed.transpose(1, 0, 2, 3, 4).reshape(nb * BIN, t)
    down_term = jnp.concatenate([early, to_rows(after(down_term[1:], mixed))], axis=1)
    mixed = to_store(mixed)
    up_grad, down_grad = sum_rows(up_term, down_term, down_blocks.shape)
    return mixed, fgrad, up_grad, down_grad


def solution(mesh):
    flat = P("tensor", "dp")
    rows = P("tensor", "dp", None)
    return jax.shard_map(
        per_device,
        mesh=mesh,
        in_specs=(flat, rows, rows, flat),
        out_specs=(flat, flat, rows, rows),
        check_vma=False,
    )
```

```python
import jax
import jax.numpy as jnp
from jax import lax
from jax.sharding import PartitionSpec as P

NB = 64
BIN = 128
BOUT = 512
J_UP = 8
J_DN = 2
F32 = jnp.float32
BF16 = jnp.bfloat16


def gelu_value(v):
    return 0.5 * v * (1.0 + lax.erf(v * 0.7071067811865476))


def gelu_slope(v):
    return (
        0.5 * (1.0 + lax.erf(v * 0.7071067811865476))
        + v * jnp.exp(-0.5 * v * v) * 0.3989422804014327
    )


DEVICES = ("dp", "tensor")


def back(pairs):
    return [(b, a) for a, b in pairs]


class Plan:
    def __init__(self):
        def index(xh, y, c, z, xl):
            return (((xh * 4 + y) * 2 + c) * 16 + z) * 2 + xl

        shuffle, mirror, weights, place = [], [], [], {}
        for z in range(16):
            for t in range(16):
                xh, y, c = t >> 3, (t >> 1) & 3, t & 1
                label = 8 * c + 4 * xh + y
                moved = (label + z) % 16
                c2, xh2, y2 = moved >> 3, (moved >> 2) & 1, moved & 3
                for xl in range(2):
                    xl2 = xl if xh2 == xh else 1 - xl
                    mid = index(xh2, y2, c2, z, xl2)
                    end = index(xh2, y2, c2, label, xl2)
                    shuffle.append((index(xh, y, c, z, xl), mid))
                    mirror.append((mid, end))
                    weights.append((index(xh2, y2, c2, z, xl), end))
                    place[label, 2 * z + xl] = end
        self.shuffle, self.mirror, self.weights = shuffle, mirror, weights
        outward = dict(back(mirror)), dict(back(shuffle))
        self.home = [(end, outward[1][mid]) for end, mid in outward[0].items()]
        self.layers = [[place[t, k] for k in range(32)] for t in range(16)]


PLAN = Plan()


def exchange(x):
    return lax.all_to_all(
        x, DEVICES, split_axis=0, concat_axis=0, tiled=True, axis_index_groups=PLAN.layers
    )


def after(x, *others):
    return lax.optimization_barrier((x,) + others)[0]


def shuffle(x):
    return lax.ppermute(x, DEVICES, PLAN.shuffle)


def mirror(x):
    return lax.ppermute(x, DEVICES, PLAN.mirror)


def unmirror(x):
    return lax.ppermute(x, DEVICES, back(PLAN.mirror))


def unshuffle(x):
    return lax.ppermute(x, DEVICES, back(PLAN.shuffle))


def to_store(x):
    return lax.ppermute(x, DEVICES, PLAN.home)


def gather_rows(up_blocks, down_blocks):
    n = lax.axis_size("dp")
    nb, ru, wu = up_blocks.shape
    both = jnp.concatenate([up_blocks, down_blocks.reshape(nb, ru, wu)], axis=0)
    sent = jnp.broadcast_to(both, (n,) + both.shape)
    got = lax.all_to_all(sent, "dp", split_axis=0, concat_axis=0, tiled=True)
    return got[:, :nb], got[:, nb:]


def whole(rows, height, width):
    n, nb = rows.shape[:2]
    rows = lax.ppermute(rows, DEVICES, PLAN.weights)
    return rows.reshape(n, nb, height // n, width).transpose(1, 0, 2, 3).reshape(nb, height, width)


def sum_rows(up_term, down_term):
    n = lax.axis_size("dp")
    nb, hu, wu = up_term.shape
    hd, wd = down_term.shape[1:]
    ru, rd = hu // n, hd // n
    u = up_term.astype(BF16).reshape(nb, n, ru, wu).transpose(1, 0, 2, 3)
    d = down_term.astype(BF16).reshape(nb, n, ru, wu).transpose(1, 0, 2, 3)
    u = lax.ppermute(u, DEVICES, back(PLAN.weights))
    d = lax.ppermute(d, DEVICES, back(PLAN.weights))
    both = jnp.concatenate([u, d], axis=1)
    got = lax.all_to_all(both, "dp", split_axis=0, concat_axis=0, tiled=True)
    s = jnp.sum(got.astype(F32), axis=0)
    return s[:nb], s[nb:].reshape(nb, rd, wd)


def per_device(features, up_blocks, down_blocks, out_cotangent):
    nb = up_blocks.shape[0]
    t = features.shape[1]
    n = NB // nb
    moved = shuffle(features)
    cot = mirror(shuffle(out_cotangent))
    up_rows, down_rows = gather_rows(up_blocks, down_blocks)
    up = whole(up_rows, BIN, BOUT)
    x_flat = mirror(after(moved, cot))
    dblock = exchange(cot.reshape(nb, n, nb, J_DN, t).transpose(1, 2, 0, 3, 4))
    x = after(x_flat, dblock).reshape(nb, BIN, t)
    pre = jnp.einsum("bkn,bkt->bnt", up, x, preferred_element_type=F32).astype(BF16)
    permuted = exchange(pre.reshape(nb, n, nb, J_UP, t).transpose(1, 2, 0, 3, 4))
    down = whole(after(down_rows, x_flat), BOUT, BIN)
    permuted = permuted.transpose(1, 0, 2, 3, 4).reshape(nb, BOUT, t)
    pf = permuted.astype(F32)
    act = gelu_value(pf).astype(BF16)
    blockout = jnp.einsum("gmc,gmt->gct", down, act, preferred_element_type=F32).astype(BF16)
    blockout = blockout.reshape(nb, n, nb, J_DN, t).transpose(1, 2, 0, 3, 4)
    mixed = exchange(blockout)
    dblock = dblock.transpose(1, 0, 2, 3, 4).reshape(nb, BIN, t)
    dact = jnp.einsum("gmc,gct->gmt", down, dblock, preferred_element_type=F32)
    dperm = (dact * gelu_slope(pf)).astype(BF16)
    dperm = dperm.reshape(nb, n, nb, J_UP, t).transpose(1, 2, 0, 3, 4)
    dpre = exchange(after(dperm, mixed))
    mixed = unmirror(mixed.transpose(1, 0, 2, 3, 4).reshape(nb * BIN, t))
    down_term = jnp.einsum("gmt,gct->gmc", act, dblock, preferred_element_type=F32)
    dpre = dpre.transpose(1, 0, 2, 3, 4).reshape(nb, BOUT, t)
    fgrad = jnp.einsum("bkn,bnt->bkt", up, dpre, preferred_element_type=F32).astype(BF16)
    fgrad = fgrad.reshape(nb * BIN, t)
    dpre = after(dpre, fgrad, mixed)
    up_term = jnp.einsum("bkt,bnt->bkn", x, dpre, preferred_element_type=F32)
    up_grad, down_grad = sum_rows(up_term, down_term)
    return unshuffle(mixed), to_store(fgrad), up_grad, down_grad


def solution(mesh):
    flat = P("tensor", "dp")
    rows = P("tensor", "dp", None)
    return jax.shard_map(
        per_device,
        mesh=mesh,
        in_specs=(flat, rows, rows, flat),
        out_specs=(flat, flat, rows, rows),
        check_vma=False,
    )
```

```python
import jax
import jax.numpy as jnp
from jax import lax
from jax.sharding import PartitionSpec as P

NB = 64
BIN = 128
BOUT = 512
J_UP = 8
J_DN = 2
F32 = jnp.float32
BF16 = jnp.bfloat16


def gelu_value(v):
    return 0.5 * v * (1.0 + lax.erf(v * 0.7071067811865476))


def gelu_slope(v):
    return (
        0.5 * (1.0 + lax.erf(v * 0.7071067811865476))
        + v * jnp.exp(-0.5 * v * v) * 0.3989422804014327
    )


DEVICES = ("dp", "tensor")


def back(pairs):
    return [(b, a) for a, b in pairs]


class Plan:
    def __init__(self):
        def index(xh, y, c, z, xl):
            return (((xh * 4 + y) * 2 + c) * 16 + z) * 2 + xl

        shuffle, mirror, weights, place = [], [], [], {}
        for z in range(16):
            for t in range(16):
                xh, y, c = t >> 3, (t >> 1) & 3, t & 1
                label = 8 * c + 4 * xh + y
                moved = (label + z) % 16
                c2, xh2, y2 = moved >> 3, (moved >> 2) & 1, moved & 3
                for xl in range(2):
                    xl2 = xl if xh2 == xh else 1 - xl
                    mid = index(xh2, y2, c2, z, xl2)
                    end = index(xh2, y2, c2, label, xl2)
                    shuffle.append((index(xh, y, c, z, xl), mid))
                    mirror.append((mid, end))
                    weights.append((index(xh2, y2, c2, z, xl), end))
                    place[label, 2 * z + xl] = end
        self.shuffle, self.mirror, self.weights = shuffle, mirror, weights
        outward = dict(back(mirror)), dict(back(shuffle))
        self.home = [(end, outward[1][mid]) for end, mid in outward[0].items()]
        self.layers = [[place[t, k] for k in range(32)] for t in range(16)]


PLAN = Plan()


def exchange(x):
    return lax.all_to_all(
        x, DEVICES, split_axis=0, concat_axis=0, tiled=True, axis_index_groups=PLAN.layers
    )


def after(x, *others):
    return lax.optimization_barrier((x,) + others)[0]


def shuffle(x):
    return lax.ppermute(x, DEVICES, PLAN.shuffle)


def mirror(x):
    return lax.ppermute(x, DEVICES, PLAN.mirror)


def unmirror(x):
    return lax.ppermute(x, DEVICES, back(PLAN.mirror))


def unshuffle(x):
    return lax.ppermute(x, DEVICES, back(PLAN.shuffle))


def to_store(x):
    return lax.ppermute(x, DEVICES, PLAN.home)


def gather_rows(up_blocks, down_blocks):
    n = lax.axis_size("dp")
    nb, ru, wu = up_blocks.shape
    both = jnp.concatenate([up_blocks, down_blocks.reshape(nb, ru, wu)], axis=0)
    sent = jnp.broadcast_to(both, (n,) + both.shape)
    got = lax.all_to_all(sent, "dp", split_axis=0, concat_axis=0, tiled=True)
    return got[:, :nb], got[:, nb:]


def whole(rows, height, width):
    n, nb = rows.shape[:2]
    rows = lax.ppermute(rows, DEVICES, PLAN.weights)
    return rows.reshape(n, nb, height // n, width).transpose(1, 0, 2, 3).reshape(nb, height, width)


def sum_rows(up_term, down_term):
    n = lax.axis_size("dp")
    nb, hu, wu = up_term.shape
    hd, wd = down_term.shape[1:]
    ru, rd = hu // n, hd // n
    u = up_term.astype(BF16).reshape(nb, n, ru, wu).transpose(1, 0, 2, 3)
    d = down_term.astype(BF16).reshape(nb, n, ru, wu).transpose(1, 0, 2, 3)
    u = lax.ppermute(u, DEVICES, back(PLAN.weights))
    d = lax.ppermute(d, DEVICES, back(PLAN.weights))
    both = jnp.concatenate([u, d], axis=1)
    got = lax.all_to_all(both, "dp", split_axis=0, concat_axis=0, tiled=True)
    s = jnp.sum(got.astype(F32), axis=0)
    return s[:nb], s[nb:].reshape(nb, rd, wd)


def per_device(features, up_blocks, down_blocks, out_cotangent):
    nb = up_blocks.shape[0]
    t = features.shape[1]
    n = NB // nb
    moved = shuffle(features)
    cot = mirror(shuffle(out_cotangent))
    up_rows, down_rows = gather_rows(up_blocks, down_blocks)
    up = whole(up_rows, BIN, BOUT)
    x_flat = mirror(after(moved, cot))
    dblock = exchange(cot.reshape(nb, n, nb, J_DN, t).transpose(1, 2, 0, 3, 4))
    x = after(x_flat, dblock).reshape(nb, BIN, t)
    pre = jnp.einsum("bkn,bkt->bnt", up, x, preferred_element_type=F32).astype(BF16)
    permuted = exchange(pre.reshape(nb, n, nb, J_UP, t).transpose(1, 2, 0, 3, 4))
    down = whole(after(down_rows, x_flat), BOUT, BIN)
    permuted = permuted.transpose(1, 0, 2, 3, 4).reshape(nb, BOUT, t)
    act = gelu_value(permuted.astype(F32)).astype(BF16)
    pf = lax.optimization_barrier(permuted).astype(F32)
    blockout = jnp.einsum("gmc,gmt->gct", down, act, preferred_element_type=F32).astype(BF16)
    blockout = blockout.reshape(nb, n, nb, J_DN, t).transpose(1, 2, 0, 3, 4)
    mixed = exchange(blockout)
    dblock = dblock.transpose(1, 0, 2, 3, 4).reshape(nb, BIN, t)
    dact = jnp.einsum("gmc,gct->gmt", down, dblock, preferred_element_type=F32)
    dperm = (dact * gelu_slope(pf)).astype(BF16)
    dperm = dperm.reshape(nb, n, nb, J_UP, t).transpose(1, 2, 0, 3, 4)
    dpre = exchange(after(dperm, mixed))
    mixed = unmirror(mixed.transpose(1, 0, 2, 3, 4).reshape(nb * BIN, t))
    down_term = jnp.einsum("gmt,gct->gmc", act, dblock, preferred_element_type=F32)
    dpre = dpre.transpose(1, 0, 2, 3, 4).reshape(nb, BOUT, t)
    fgrad = jnp.einsum("bkn,bnt->bkt", up, dpre, preferred_element_type=F32).astype(BF16)
    fgrad = fgrad.reshape(nb * BIN, t)
    dpre = after(dpre, fgrad, mixed)
    up_term = jnp.einsum("bkt,bnt->bkn", x, dpre, preferred_element_type=F32)
    up_grad, down_grad = sum_rows(up_term, down_term)
    return unshuffle(mixed), to_store(fgrad), up_grad, down_grad


def solution(mesh):
    flat = P("tensor", "dp")
    rows = P("tensor", "dp", None)
    return jax.shard_map(
        per_device,
        mesh=mesh,
        in_specs=(flat, rows, rows, flat),
        out_specs=(flat, flat, rows, rows),
        check_vma=False,
    )
```

```python
import jax
import jax.numpy as jnp
from jax import lax
from jax.sharding import PartitionSpec as P

NB = 64
BIN = 128
BOUT = 512
J_UP = 8
J_DN = 2
F32 = jnp.float32
BF16 = jnp.bfloat16


def gelu_value(v):
    return 0.5 * v * (1.0 + lax.erf(v * 0.7071067811865476))


def gelu_slope(v):
    return (
        0.5 * (1.0 + lax.erf(v * 0.7071067811865476))
        + v * jnp.exp(-0.5 * v * v) * 0.3989422804014327
    )


DEVICES = ("dp", "tensor")


def back(pairs):
    return [(b, a) for a, b in pairs]


class Plan:
    def __init__(self):
        def index(xh, y, c, z, xl):
            return (((xh * 4 + y) * 2 + c) * 16 + z) * 2 + xl

        shuffle, mirror, weights, place = [], [], [], {}
        for z in range(16):
            for t in range(16):
                xh, y, c = t >> 3, (t >> 1) & 3, t & 1
                label = 8 * c + 4 * xh + y
                moved = (label + z) % 16
                c2, xh2, y2 = moved >> 3, (moved >> 2) & 1, moved & 3
                for xl in range(2):
                    xl2 = xl if xh2 == xh else 1 - xl
                    mid = index(xh2, y2, c2, z, xl2)
                    end = index(xh2, y2, c2, label, xl2)
                    shuffle.append((index(xh, y, c, z, xl), mid))
                    mirror.append((mid, end))
                    weights.append((index(xh2, y2, c2, z, xl), end))
                    place[label, 2 * z + xl] = end
        self.shuffle, self.mirror, self.weights = shuffle, mirror, weights
        outward = dict(back(mirror)), dict(back(shuffle))
        self.home = [(end, outward[1][mid]) for end, mid in outward[0].items()]
        self.layers = [[place[t, k] for k in range(32)] for t in range(16)]


PLAN = Plan()


def exchange(x):
    return lax.all_to_all(
        x, DEVICES, split_axis=0, concat_axis=0, tiled=True, axis_index_groups=PLAN.layers
    )


def after(x, *others):
    return lax.optimization_barrier((x,) + others)[0]


def shuffle(x):
    return lax.ppermute(x, DEVICES, PLAN.shuffle)


def mirror(x):
    return lax.ppermute(x, DEVICES, PLAN.mirror)


def unmirror(x):
    return lax.ppermute(x, DEVICES, back(PLAN.mirror))


def unshuffle(x):
    return lax.ppermute(x, DEVICES, back(PLAN.shuffle))


def to_store(x):
    return lax.ppermute(x, DEVICES, PLAN.home)


def gather_rows(up_blocks, down_blocks):
    n = lax.axis_size("dp")
    nb, ru, wu = up_blocks.shape
    both = jnp.concatenate([up_blocks, down_blocks.reshape(nb, ru, wu)], axis=0)
    sent = jnp.broadcast_to(both, (n,) + both.shape)
    got = lax.all_to_all(sent, "dp", split_axis=0, concat_axis=0, tiled=True)
    return got[:, :nb], got[:, nb:]


def whole(rows, height, width):
    n, nb = rows.shape[:2]
    rows = lax.ppermute(rows, DEVICES, PLAN.weights)
    return rows.reshape(n, nb, height // n, width).transpose(1, 0, 2, 3).reshape(nb, height, width)


def sum_rows(up_term, down_term):
    n = lax.axis_size("dp")
    nb, hu, wu = up_term.shape
    hd, wd = down_term.shape[1:]
    ru, rd = hu // n, hd // n
    u = up_term.astype(BF16).reshape(nb, n, ru, wu).transpose(1, 0, 2, 3)
    d = down_term.astype(BF16).reshape(nb, n, ru, wu).transpose(1, 0, 2, 3)
    u = lax.ppermute(u, DEVICES, back(PLAN.weights))
    d = lax.ppermute(d, DEVICES, back(PLAN.weights))
    both = jnp.concatenate([u, d], axis=1)
    got = lax.all_to_all(both, "dp", split_axis=0, concat_axis=0, tiled=True)
    s = jnp.sum(got.astype(F32), axis=0)
    return s[:nb], s[nb:].reshape(nb, rd, wd)


def per_device(features, up_blocks, down_blocks, out_cotangent):
    nb = up_blocks.shape[0]
    t = features.shape[1]
    n = NB // nb
    moved = shuffle(features)
    cot = mirror(shuffle(out_cotangent))
    up_rows, down_rows = gather_rows(up_blocks, down_blocks)
    up = whole(up_rows, BIN, BOUT)
    x_flat = mirror(after(moved, cot))
    dblock = exchange(cot.reshape(nb, n, nb, J_DN, t).transpose(1, 2, 0, 3, 4))
    x = after(x_flat, dblock).reshape(nb, BIN, t)
    pre = jnp.einsum("bkn,bkt->bnt", up, x, preferred_element_type=F32).astype(BF16)
    permuted = exchange(pre.reshape(nb, n, nb, J_UP, t).transpose(1, 2, 0, 3, 4))
    down = whole(after(down_rows, x_flat), BOUT, BIN)
    permuted = permuted.transpose(1, 0, 2, 3, 4).reshape(nb, BOUT, t)
    act = gelu_value(permuted.astype(F32)).astype(BF16)
    pf = lax.optimization_barrier(permuted).astype(F32)
    blockout = jnp.einsum("gmc,gmt->gct", down, act, preferred_element_type=F32).astype(BF16)
    blockout = blockout.reshape(nb, n, nb, J_DN, t).transpose(1, 2, 0, 3, 4)
    mixed = exchange(blockout)
    dblock = dblock.transpose(1, 0, 2, 3, 4).reshape(nb, BIN, t)
    dact = jnp.einsum("gmc,gct->gmt", down, dblock, preferred_element_type=F32)
    dperm = (dact * gelu_slope(pf)).astype(BF16)
    dperm = dperm.reshape(nb, n, nb, J_UP, t).transpose(1, 2, 0, 3, 4)
    dpre = exchange(after(dperm, mixed))
    mixed = unmirror(mixed.transpose(1, 0, 2, 3, 4).reshape(nb * BIN, t))
    down_term = jnp.einsum("gmt,gct->gmc", act, dblock, preferred_element_type=F32).astype(BF16)
    down_term = after(down_term, mixed)
    dpre = dpre.transpose(1, 0, 2, 3, 4).reshape(nb, BOUT, t)
    fgrad = jnp.einsum("bkn,bnt->bkt", up, dpre, preferred_element_type=F32).astype(BF16)
    fgrad = fgrad.reshape(nb * BIN, t)
    dpre = after(dpre, fgrad)
    up_term = jnp.einsum("bkt,bnt->bkn", x, dpre, preferred_element_type=F32)
    up_grad, down_grad = sum_rows(up_term, down_term)
    return unshuffle(mixed), to_store(fgrad), up_grad, down_grad


def solution(mesh):
    flat = P("tensor", "dp")
    rows = P("tensor", "dp", None)
    return jax.shard_map(
        per_device,
        mesh=mesh,
        in_specs=(flat, rows, rows, flat),
        out_specs=(flat, flat, rows, rows),
        check_vma=False,
    )
```
